32 devices in a mesh: grp: 2 (over x), row: 16 (over z, y, core).
Axes of the slice: x: 2, y: 2, z: 4, core: 2. Of those that a mesh axis runs over, the one named last changes fastest.
Arguments:
- geometry: float32 [9, 16384], P(None, ('grp', 'row')), parts along dimension 1, as said below
- emission: float32 [16, 16384], P(None, ('grp', 'row')), parts along dimension 1, may hold values from 0.1 to 10
- reflect: float32 [16384], P(('grp', 'row')), parts along dimension 0, may hold values from 0.2 to 0.8
- occlusion: int32 [1024, 256], P(('grp', 'row')), parts along dimension 0, may hold values from 0 to 65535
- pair_recv: int32 [1024], P(('grp', 'row')), parts along dimension 0, may hold values from 0 to 31, as said below
- pair_src: int32 [1024], P(('grp', 'row')), parts along dimension 0, may hold values from 0 to 1
- pair_count: int32 [32], P(('grp', 'row')), parts along dimension 0, may hold values from 8 to 32, as said below
Outputs:
- radiosity: float32 [16, 16384], P(None, ('grp', 'row')), parts along dimension 1
- row_sums: float32 [16384], P(('grp', 'row')), parts along dimension 0
The draws below stay inside these ranges and needn't reach their ends.
There are 2 independent parts, one for each index of `grp`. The reference program is written for one: setup_inputs(seed, part) draws one part's arguments, and reference() takes and returns one part's arrays. A program takes and returns all parts, laid end to end along the dimension named above; each array names one. Nothing has to cross between parts.
Inputs may be any that keep to these rules, and one draw needn't show every extreme that they name: `pair_recv`: in each index of row the 32 slots name distinct receiving tiles. `pair_count`: some index of row has all 32 slots live in every draw. `geometry`: edges are never parallel; every area is 0.2 or more.
All inputs are finite; a program needn't handle non-finite values.
Results may differ from the reference program's by a relative error of at most 0.0003.
Values sent between devices are 32-bit elements; how exact they have to be, the bound alone decides.
No kernel may reach another device: no remote copies, remote signals or barrier semaphores. Data moves between devices by JAX's collectives and lax.ppermute only.
A program may use at most 64 MiB of HBM per device.

```python
import math
import jax
import jax.numpy as jnp
from jax import lax

TILE = 256
GROUPS = 16
HOURS = 16
BOUNCES = 2
TILES_DEV = 2
PAIRS_DEV = 32
TILES = 32
PATCHES = 8192
PAIRS = 512
N_ROW = 16


def draw_geometry(key, part):
    count = TILES * TILE
    keys = jax.random.split(jax.random.fold_in(key, 11), 5)
    span = 5.0
    lo_side = 0.5
    hi_side = 2.0
    box = jnp.array([span, span, span / 2.0], jnp.float32)[:, None]
    corner = jax.random.uniform(keys[0], (3, count), jnp.float32) * box
    theta = jax.random.uniform(keys[1], (count,), jnp.float32, -math.pi, math.pi)
    width = jnp.exp(jax.random.uniform(keys[2], (count,), jnp.float32, math.log(lo_side), math.log(hi_side)))
    height = jnp.exp(jax.random.uniform(keys[3], (count,), jnp.float32, math.log(lo_side), math.log(hi_side)))
    tilt = jax.random.uniform(keys[4], (2, count), jnp.float32, -1.0, 1.0)
    edge_u = jnp.stack([width * jnp.cos(theta), width * jnp.sin(theta), 0.1 * width * tilt[0]])
    edge_v = jnp.stack([0.2 * height * tilt[1], -0.2 * height * tilt[0], height])
    return jnp.concatenate([corner, edge_u, edge_v], axis=0).astype(jnp.float32)


def draw_pair_recv(key, part):
    keys = jax.random.split(jax.random.fold_in(key, 23), N_ROW)
    rows = jax.vmap(lambda k: jax.random.permutation(k, TILES)[:PAIRS_DEV])(keys)
    return rows.reshape(-1).astype(jnp.int32)


def draw_pair_count(key, part):
    base_key = jax.random.fold_in(key, 37)
    full_key = jax.random.fold_in(key, 41)
    base = jax.random.randint(base_key, (N_ROW,), PAIRS_DEV // 4, PAIRS_DEV // 2 + 1)
    full = jax.random.randint(full_key, (), 0, N_ROW)
    return jnp.where(jnp.arange(N_ROW) == full, PAIRS_DEV, base).astype(jnp.int32)


def touch_ends(values, own_key, least, top_value):
    longest = values.shape.index(max(values.shape))
    spots = []
    for shift in (0, 1):
        where = [jax.random.randint(jax.random.fold_in(own_key, axis), (), 0, length) for axis, length in enumerate(values.shape)]
        where[longest] = (where[longest] + shift) % values.shape[longest]
        spots.append(tuple(where))
    return values.at[spots[0]].set(least).at[spots[1]].set(top_value)


def level_of(key, shape, pieces, smallest, largest):
    def one(dim, shards_of):
        steps = jax.random.uniform(jax.random.fold_in(jax.random.fold_in(key, 6), dim), (shards_of,), jnp.float32, smallest / len(pieces), largest / len(pieces))
        return jnp.repeat(jnp.exp(steps), shape[dim] // shards_of).reshape((-1,) + (1,) * (len(shape) - dim - 1))

    factor_of = one(*pieces[0])
    for cut in pieces[1:]:
        factor_of = factor_of * one(*cut)
    return factor_of


def setup_inputs(seed: int = 0, part: int = 0) -> dict:
    key_list = jax.random.split(jax.random.key(seed), 8)
    part_keys = jax.random.split(jax.random.fold_in(key_list[7], part), 8)
    geometry = draw_geometry(jax.random.fold_in(jax.random.fold_in(key_list[7], part), 71), part)
    emission = jnp.clip(jnp.exp(math.log(10.0) - 4.6051702 * jax.random.uniform(part_keys[1], (HOURS, PATCHES), jnp.float32) ** level_of(part_keys[1], (HOURS, PATCHES), ((1, 16),), -0.2, 0.2)), 0.1, 10.0)
    reflect = jnp.clip(0.2 + 0.6 * jax.random.uniform(part_keys[2], (PATCHES,), jnp.float32) ** level_of(part_keys[2], (PATCHES,), ((0, 16),), -0.2, 0.2), 0.2, 0.8)
    occlusion = touch_ends(jax.random.randint(part_keys[3], (PAIRS, TILE), 0, 65536), jax.random.fold_in(part_keys[3], 1), 0, 65535).astype(jnp.int32)
    pair_recv = draw_pair_recv(jax.random.fold_in(jax.random.fold_in(key_list[7], part), 71), part)
    pair_src = touch_ends(jax.random.randint(part_keys[5], (PAIRS,), 0, TILES_DEV), jax.random.fold_in(part_keys[5], 1), 0, TILES_DEV - 1).astype(jnp.int32)
    pair_count = draw_pair_count(jax.random.fold_in(jax.random.fold_in(key_list[7], part), 71), part)
    return {"geometry": geometry, "emission": emission, "reflect": reflect, "occlusion": occlusion, "pair_recv": pair_recv, "pair_src": pair_src, "pair_count": pair_count}


def patch_frame(geometry):
    corner = geometry[0:3]
    edge_u = geometry[3:6]
    edge_v = geometry[6:9]
    cross = jnp.stack([edge_u[1] * edge_v[2] - edge_u[2] * edge_v[1], edge_u[2] * edge_v[0] - edge_u[0] * edge_v[2], edge_u[0] * edge_v[1] - edge_u[1] * edge_v[0]])
    area = jnp.sqrt(lax.optimization_barrier(jnp.sum(cross * cross, axis=0)))
    normal = cross / area
    points = jnp.stack([corner + s * edge_u + t * edge_v for s in (0.25, 0.75) for t in (0.25, 0.75)])
    return (points, normal, area)

def view_block(recv_points, recv_normal, src_points, src_normal, src_area, words, group):
    diffs = [src_points[None, :, c, None, :] - recv_points[:, None, c, :, None] for c in range(3)]
    dist_sq = diffs[0] * diffs[0] + diffs[1] * diffs[1] + diffs[2] * diffs[2]
    cos_recv = recv_normal[0][:, None] * diffs[0] + recv_normal[1][:, None] * diffs[1] + recv_normal[2][:, None] * diffs[2]
    cos_src = -(src_normal[0][None, :] * diffs[0] + src_normal[1][None, :] * diffs[1] + src_normal[2][None, :] * diffs[2])
    spread_sq = dist_sq + src_area[None, :] / 4.0
    kernel = jnp.maximum(cos_recv, 0.0) * jnp.maximum(cos_src, 0.0) / (math.pi * spread_sq * spread_sq)
    summed = lax.optimization_barrier(jnp.sum(kernel, axis=(0, 1)))
    visible = jnp.bitwise_and(jnp.right_shift(words[:, None], group[None, :]), 1).astype(jnp.float32)
    return src_area[None, :] / 16.0 * visible * summed

def reference(geometry, emission, reflect, occlusion, pair_recv, pair_src, pair_count):
    points, normal, area = patch_frame(geometry)
    tiles = TILES_DEV * N_ROW
    slots = jnp.arange(PAIRS, dtype=jnp.int32)
    owner = slots // PAIRS_DEV
    source_tile = (owner * TILES_DEV + pair_src).astype(jnp.int32)
    live = (slots % PAIRS_DEV < pair_count[owner]).astype(jnp.float32)
    group = (jnp.arange(TILE, dtype=jnp.int32) // (TILE // GROUPS)).astype(jnp.int32)

    def one_block(k):
        r_start = (pair_recv[k] * TILE).astype(jnp.int32)
        s_start = (source_tile[k] * TILE).astype(jnp.int32)
        block = view_block(lax.dynamic_slice_in_dim(points, r_start, TILE, 2), lax.dynamic_slice_in_dim(normal, r_start, TILE, 1), lax.dynamic_slice_in_dim(points, s_start, TILE, 2), lax.dynamic_slice_in_dim(normal, s_start, TILE, 1), lax.dynamic_slice_in_dim(area, s_start, TILE, 0), occlusion[k], group)
        return block * live[k]
    blocks = lax.map(one_block, slots)
    row_sums = jnp.zeros((tiles, TILE), jnp.float32).at[pair_recv].add(lax.optimization_barrier(jnp.sum(blocks, axis=2))).reshape(-1)
    scale = reflect / jnp.maximum(row_sums, 1.0)
    radiosity = emission
    for bounce in range(BOUNCES):
        source = radiosity.reshape(HOURS, tiles, TILE)[:, source_tile]
        contrib = jnp.einsum('hkj,kij->khi', source, blocks, precision=lax.Precision.HIGHEST)
        irr = jnp.zeros((tiles, HOURS, TILE), jnp.float32).at[pair_recv].add(contrib)
        irr = jnp.transpose(irr, (1, 0, 2)).reshape(HOURS, tiles * TILE)
        radiosity = emission + scale[None, :] * irr
    return (radiosity, row_sums)
```

```python
import math

import jax
import jax.numpy as jnp
from jax import lax
from jax.experimental import pallas as pl
from jax.experimental.pallas import tpu as pltpu
from jax.sharding import PartitionSpec as P

TILE = 256
GROUPS = 16
HOURS = 16
CH = 32
N_CH = TILE // CH
SPLIT_K = 48
BF16 = jnp.bfloat16
F32 = jnp.float32

ROW_OCC = 16
ROW_GEO = 32
ROW_CODE = 41
ROWS = 42


def to_bf16(x):
    return x.astype(BF16).astype(F32)


def split3(x, narrow=to_bf16):
    hi = narrow(x)
    rest = x - hi
    mid = narrow(rest)
    return hi, mid, rest - mid


def split2(x):
    hi = x.astype(BF16)
    return hi, (x - hi.astype(F32)).astype(BF16)


def cross_of(u, v):
    return (
        u[1] * v[2] - u[2] * v[1],
        u[2] * v[0] - u[0] * v[2],
        u[0] * v[1] - u[1] * v[0],
    )


def dot3(a, b):
    return a[0] * b[0] + a[1] * b[1] + a[2] * b[2]


def frame(geo, origin):
    corner = [geo[c] - origin[c] for c in range(3)]
    u = [geo[3 + c] for c in range(3)]
    v = [geo[6 + c] for c in range(3)]
    centre = [corner[c] + 0.5 * (u[c] + v[c]) for c in range(3)]
    e1 = [0.25 * (u[c] + v[c]) for c in range(3)]
    e2 = [0.25 * (u[c] - v[c]) for c in range(3)]
    cross = cross_of(u, v)
    area = jnp.sqrt(dot3(cross, cross))
    normal = [cross[c] / area for c in range(3)]
    offsets = [e1, [-x for x in e1], e2, [-x for x in e2]]
    return centre, offsets, normal, area


def recv_factors(geometry, origin):
    geo = [geometry[c] for c in range(9)]
    centre, offsets, normal, _ = frame(geo, origin)
    one = jnp.ones_like(centre[0])

    def stack(rows):
        hi, mid, lo = split3(jnp.stack(rows), lambda x: lax.reduce_precision(x, 8, 7))
        return jnp.concatenate([hi, hi, hi, mid, mid, lo], 0).astype(BF16)

    points = jnp.stack(
        [
            stack(
                [centre[c] + a[c] for c in range(3)]
                + list(a)
                + [one, dot3(a, a) + 2.0 * dot3(centre, a)]
            )
            for a in offsets
        ]
    )
    n = geometry.shape[1]
    points = points.reshape(4, SPLIT_K, n // CH, CH).transpose(2, 0, 3, 1)
    points = points.reshape(n // CH, 4 * CH, SPLIT_K)
    centres = stack(list(normal) + [-dot3(normal, centre)] + list(centre) + [one]).T
    return points, centres


def source_factors(geo_ref, j, start, origin, rhs1, rhs2):
    lanes = pl.ds(start, TILE)
    geo = [geo_ref[j, ROW_GEO + c : ROW_GEO + c + 1, lanes] for c in range(9)]
    centre, offsets, normal, area = frame(geo, origin)
    one = jnp.ones_like(area)
    zero = jnp.zeros_like(area)

    def put(ref, col, rows):
        hi, mid, lo = split3(jnp.concatenate(rows, 0))
        ref[:, col * TILE : (col + 1) * TILE] = jnp.concatenate(
            [hi, mid, lo, hi, mid, hi], 0
        ).astype(BF16)

    m2 = [-2.0 * x for x in centre]
    for q, b in enumerate(offsets):
        put(
            rhs1,
            q,
            [-2.0 * x for x in b]
            + m2
            + [dot3(b, b) + 2.0 * dot3(centre, b) + 0.25 * area, one],
        )
    put(rhs1, 4, list(normal) + [zero] * 3 + [-dot3(normal, centre), zero])
    weight = area * (1.0 / (16.0 * math.pi))
    for q, b in enumerate(offsets):
        put(
            rhs2,
            q,
            [(centre[c] + b[c]) * weight for c in range(3)] + [weight] + [zero] * 4,
        )
    for c in range(3):
        put(
            rhs2,
            4 + c,
            [zero] * 4 + [-one if c == k else zero for k in range(3)] + [centre[c]],
        )


def mm(a, b):
    return lax.dot_general(a, b, (((1,), (0,)), ((), ())), preferred_element_type=F32)


def mm_t(a, b):
    return lax.dot_general(a, b, (((1,), (1,)), ((), ())), preferred_element_type=F32)


def inverse_square(t):
    square = t * t
    x = pl.reciprocal(square, approx=True)
    return x * (2.0 - square * x)


def block_kernel(
    code, origin_ref, pay, left1, left2, words_t, refl, emis,
    blocks, out_b, out_sums, out_scale,
    rhs1, rhs2, word_s, acc_hi, acc_lo, buf, sem,
):
    n_dev = pay.shape[0]
    origin = [origin_ref[c] for c in range(3)]
    acc_hi[...] = jnp.zeros_like(acc_hi)
    acc_lo[...] = jnp.zeros_like(acc_lo)
    lane = lax.broadcasted_iota(jnp.int32, (1, TILE), 1)
    group_bit = jnp.left_shift(1, lane // (TILE // GROUPS))

    def out_copy(slot, k):
        return pltpu.make_async_copy(buf.at[slot], blocks.at[k], sem.at[slot])

    def pair(k, done):
        r = k // n_dev
        j = k - r * n_dev
        value = code[j, r]

        @pl.when(value > 0)
        def _():
            slot = done & 1

            @pl.when(done >= 2)
            def _():
                out_copy(slot, k).wait()

            src = (value - 1) & 1
            source_factors(pay, j, pl.multiple_of(src * TILE, TILE), origin, rhs1, rhs2)
            n_sel = words_t.shape[2]
            row = lax.broadcasted_iota(jnp.int32, (n_sel, 128), 0)
            pick = jnp.where(row == j, 256.0, jnp.where(row == j + n_dev, 1.0, 0.0))
            word_s[...] = mm(words_t[r], pick.astype(BF16)).astype(jnp.int32)

            def chunk(c, carry):
                rows = pl.ds(pl.multiple_of(c * CH, CH), CH)
                lhs2 = left2[pl.ds(pl.multiple_of(r * TILE + c * CH, CH), CH), :]
                lhs1 = left1[r * N_CH + c]
                d = [mm(lhs2, rhs2[:, (4 + x) * TILE : (5 + x) * TILE]) for x in range(3)]
                s = d[0] * d[0] + d[1] * d[1] + d[2] * d[2]
                facing = jnp.maximum(mm(lhs1, rhs1[:, 4 * TILE : 5 * TILE]), 0.0)
                total = None
                for q in range(4):
                    cols = slice(q * TILE, (q + 1) * TILE)
                    rest = mm(lhs1, rhs1[:, cols])
                    part = None
                    for p in range(4):
                        pr = slice(p * CH, (p + 1) * CH)
                        term = facing[pr] * inverse_square(s + rest[pr])
                        part = term if part is None else part + term
                    a = jnp.maximum(mm(lhs2, rhs2[:, cols]), 0.0) * part
                    total = a if total is None else total + a
                w = word_s[rows, :]
                w = jnp.concatenate([w, w], 1)
                total = jnp.where((w & group_bit) != 0, total, 0.0)
                hi, lo = split2(total)
                buf[slot, 0, rows, :] = hi
                buf[slot, 1, rows, :] = lo
                return carry

            lax.fori_loop(0, N_CH, chunk, 0)
            out_copy(slot, k).start()
            x = pay[j, 0:HOURS, pl.ds(pl.multiple_of(src * TILE, TILE), TILE)]
            x_hi, x_lo = split2(x)
            ones = jnp.ones((16, TILE), BF16)
            acc_hi[r] += mm_t(jnp.concatenate([x_hi, x_lo, ones], 0), buf[slot, 0])
            acc_lo[r] += mm_t(jnp.concatenate([x_hi, ones], 0), buf[slot, 1])

        return done + (value > 0).astype(jnp.int32)

    done = lax.fori_loop(0, 2 * n_dev, pair, jnp.int32(0))
    for back in (1, 2):

        @pl.when(done >= back)
        def _():
            out_copy((done - back) & 1, 0).wait()

    for r in range(2):
        cols = slice(r * TILE, (r + 1) * TILE)
        irr = acc_hi[r, 0:16] + acc_hi[r, 16:32] + acc_lo[r, 0:16]
        sums = acc_hi[r, 32:33] + acc_lo[r, 16:17]
        scale = refl[:, cols] / jnp.maximum(sums, 1.0)
        out_sums[:, cols] = sums
        out_scale[:, cols] = scale
        out_b[:, cols] = emis[:, cols] + scale * irr


def bounce_kernel(code, field, blocks, scale, emis, out, buf, sem, acc):
    n_dev = field.shape[0]
    acc[...] = jnp.zeros_like(acc)

    def copy(k):
        return pltpu.make_async_copy(blocks.at[k], buf.at[k], sem.at[k])

    def live(k):
        r = k // n_dev
        return code[k - r * n_dev, r]

    def begin(k, carry):
        @pl.when(live(k) > 0)
        def _():
            copy(k).start()

        return carry

    lax.fori_loop(0, 2 * n_dev, begin, 0)

    def pair(k, carry):
        value = live(k)

        @pl.when(value > 0)
        def _():
            r = k // n_dev
            j = k - r * n_dev
            src = (value - 1) & 1
            x_hi, x_lo = split2(field[j, :, pl.ds(pl.multiple_of(src * TILE, TILE), TILE)])
            both = jnp.concatenate([x_hi, x_lo], 0)
            copy(k).wait()
            first = mm_t(both, buf[k, 0])
            acc[r] += first[0:16] + first[16:32] + mm_t(x_hi, buf[k, 1])

        return carry

    lax.fori_loop(0, 2 * n_dev, pair, 0)
    for r in range(2):
        cols = slice(r * TILE, (r + 1) * TILE)
        out[:, cols] = emis[:, cols] + scale[:, cols] * acc[r]


def gather_rounds(x, n_dev):
    held = x[None]
    step = n_dev // 2
    while step:
        other = lax.ppermute(held, "row", [(i, i ^ step) for i in range(n_dev)])
        held = jnp.concatenate([held, other], 0)
        step //= 2
    return held


def on_device(geometry, emission, reflect, occlusion, pair_recv, pair_src, pair_count):
    width = geometry.shape[1]
    slots = pair_recv.shape[0]
    n_dev = lax.axis_size("row")
    own = width // TILE
    me = lax.axis_index("row")

    tiles = jnp.arange(width, dtype=jnp.int32)
    slot = jnp.arange(slots, dtype=jnp.int32)
    is_slot = (pair_recv[:, None] == tiles[None, :]) & (slot < pair_count[0])[:, None]
    code = jnp.sum(jnp.where(is_slot, (2 * slot + pair_src + 1)[:, None], 0), 0)
    half = slots // 2
    words = jnp.concatenate([occlusion[:half], occlusion[half:]], 1)
    payload = jnp.concatenate(
        [emission, words.astype(F32), geometry, code.astype(F32)[None]], 0
    )
    pay = gather_rounds(payload, n_dev)

    origin = geometry[0:3, 0]
    left1, left2 = recv_factors(geometry, origin)

    codes = lax.dynamic_slice_in_dim(pay[:, ROW_CODE], me * own, own, 1).astype(jnp.int32)
    place = jnp.maximum(codes - 1, 0) // 2
    table = pay[:, ROW_OCC : ROW_OCC + half]
    table = jnp.concatenate([table[:, :, :TILE], table[:, :, TILE:]], 1)
    word = jnp.take_along_axis(table, place[:, :, None], axis=1)
    word = word.transpose(1, 2, 0)
    high = jnp.floor(word * (1.0 / 256.0))
    words_t = jnp.concatenate([high, word - 256.0 * high], 2).astype(BF16)

    vmem = pl.BlockSpec(memory_space=pltpu.VMEM)
    smem = pl.BlockSpec(memory_space=pltpu.SMEM)
    hbm = pl.BlockSpec(memory_space=pl.ANY)
    pairs = own * n_dev
    blocks, field, sums, scale = pl.pallas_call(
        block_kernel,
        out_shape=(
            jax.ShapeDtypeStruct((pairs, 2, TILE, TILE), BF16),
            jax.ShapeDtypeStruct((HOURS, width), F32),
            jax.ShapeDtypeStruct((1, width), F32),
            jax.ShapeDtypeStruct((1, width), F32),
        ),
        in_specs=[smem, smem] + [vmem] * 6,
        out_specs=(hbm, vmem, vmem, vmem),
        scratch_shapes=[
            pltpu.VMEM((SPLIT_K, 5 * TILE), BF16),
            pltpu.VMEM((SPLIT_K, 7 * TILE), BF16),
            pltpu.VMEM((TILE, 128), jnp.int32),
            pltpu.VMEM((2, 48, TILE), F32),
            pltpu.VMEM((2, 32, TILE), F32),
            pltpu.VMEM((2, 2, TILE, TILE), BF16),
            pltpu.SemaphoreType.DMA((2,)),
        ],
        name="view_blocks",
    )(codes, origin, pay, left1, left2, words_t, reflect[None], emission)

    fields = gather_rounds(field, n_dev)
    radiosity = pl.pallas_call(
        bounce_kernel,
        out_shape=jax.ShapeDtypeStruct((HOURS, width), F32),
        in_specs=[smem, vmem, hbm, vmem, vmem],
        out_specs=vmem,
        scratch_shapes=[
            pltpu.VMEM((pairs, 2, TILE, TILE), BF16),
            pltpu.SemaphoreType.DMA((pairs,)),
            pltpu.VMEM((2, HOURS, TILE), F32),
        ],
        name="second_bounce",
    )(codes, fields, blocks, scale, emission)
    return (radiosity, sums[0])


def solution(mesh):
    placed = (
        P(None, ("grp", "row")),
        P(None, ("grp", "row")),
        P(("grp", "row")),
        P(("grp", "row"), None),
        P(("grp", "row")),
        P(("grp", "row")),
        P(("grp", "row")),
    )
    return jax.shard_map(
        on_device,
        mesh=mesh,
        in_specs=placed,
        out_specs=(P(None, ("grp", "row")), P(("grp", "row"))),
        check_vma=False,
    )
```

```python
import math

import jax
import jax.numpy as jnp
from jax import lax
from jax.experimental import pallas as pl
from jax.experimental.pallas import tpu as pltpu
from jax.sharding import PartitionSpec as P

TILE = 256
GROUPS = 16
HOURS = 16
CH = 32
N_CH = TILE // CH
SPLIT_K = 48
BF16 = jnp.bfloat16
F32 = jnp.float32

ROW_OCC = 16
ROW_GEO = 32
ROW_CODE = 41
ROWS = 48


def to_bf16(x):
    return x.astype(BF16).astype(F32)


def split3(x, narrow=to_bf16):
    hi = narrow(x)
    rest = x - hi
    mid = narrow(rest)
    return hi, mid, rest - mid


def split2(x):
    hi = x.astype(BF16)
    return hi, (x - hi.astype(F32)).astype(BF16)


def cross_of(u, v):
    return (
        u[1] * v[2] - u[2] * v[1],
        u[2] * v[0] - u[0] * v[2],
        u[0] * v[1] - u[1] * v[0],
    )


def dot3(a, b):
    return a[0] * b[0] + a[1] * b[1] + a[2] * b[2]


def frame(geo, origin):
    corner = [geo[c] - origin[c] for c in range(3)]
    u = [geo[3 + c] for c in range(3)]
    v = [geo[6 + c] for c in range(3)]
    centre = [corner[c] + 0.5 * (u[c] + v[c]) for c in range(3)]
    e1 = [0.25 * (u[c] + v[c]) for c in range(3)]
    e2 = [0.25 * (u[c] - v[c]) for c in range(3)]
    cross = cross_of(u, v)
    area = jnp.sqrt(dot3(cross, cross))
    normal = [cross[c] / area for c in range(3)]
    offsets = [e1, [-x for x in e1], e2, [-x for x in e2]]
    return centre, offsets, normal, area


def recv_kernel(geo_ref, left1, left2):
    geo = [geo_ref[c : c + 1] for c in range(9)]
    origin = [geo[c][:, 0:1] for c in range(3)]
    centre, offsets, normal, _ = frame(geo, origin)
    one = jnp.ones_like(centre[0])
    zero = jnp.zeros_like(one)

    def columns(rows):
        hi, mid, lo = split3(jnp.concatenate(rows, 0))
        pad = [jnp.zeros_like(hi)] * ((128 - SPLIT_K) // 8)
        wide = jnp.concatenate([hi, hi, hi, mid, mid, lo] + pad, 0)
        return jnp.transpose(wide)[:, :SPLIT_K].astype(BF16)

    for p, a in enumerate(offsets):
        rows = [centre[c] + a[c] for c in range(3)] + list(a)
        rows += [one, dot3(a, a) + 2.0 * dot3(centre, a)]
        cols = columns(rows)
        for c in range(left1.shape[0]):
            left1[c, p * CH : (p + 1) * CH, :] = cols[c * CH : (c + 1) * CH]
    left2[...] = columns(list(normal) + [-dot3(normal, centre)] + list(centre) + [one])


def recv_factors(geometry):
    width = geometry.shape[1]
    vmem = pl.BlockSpec(memory_space=pltpu.VMEM)
    return pl.pallas_call(
        recv_kernel,
        out_shape=(
            jax.ShapeDtypeStruct((width // CH, 4 * CH, SPLIT_K), BF16),
            jax.ShapeDtypeStruct((width, SPLIT_K), BF16),
        ),
        in_specs=[vmem],
        out_specs=(vmem, vmem),
        cost_estimate=pl.CostEstimate(flops=200000, bytes_accessed=400000, transcendentals=1024),
        name="recv_factors",
    )(geometry)


def pack_kernel(recv, src, count, geo, emis, occ, out):
    slots = occ.shape[0]
    out[0:HOURS, :] = emis[...]
    words = occ[...].astype(F32)
    out[ROW_OCC : ROW_OCC + slots // 2, 0:TILE] = words[: slots // 2]
    out[ROW_OCC : ROW_OCC + slots // 2, TILE:] = words[slots // 2 :]
    out[ROW_GEO : ROW_GEO + 9, :] = geo[...]
    lane = lax.broadcasted_iota(jnp.int32, (1, out.shape[1]), 1)

    def slot(k, code):
        here = (lane == recv[k]) & (k < count[0])
        return jnp.where(here, 2 * k + src[k] + 1, code)

    code = lax.fori_loop(0, slots, slot, jnp.zeros_like(lane), unroll=8)
    out[ROW_CODE : ROW_CODE + 1, :] = code.astype(F32)
    out[ROW_CODE + 1 :, :] = jnp.zeros((ROWS - ROW_CODE - 1, out.shape[1]), F32)


def pack(geometry, emission, occlusion, pair_recv, pair_src, pair_count):
    vmem = pl.BlockSpec(memory_space=pltpu.VMEM)
    smem = pl.BlockSpec(memory_space=pltpu.SMEM)
    return pl.pallas_call(
        pack_kernel,
        out_shape=jax.ShapeDtypeStruct((ROWS, geometry.shape[1]), F32),
        in_specs=[smem] * 3 + [vmem] * 3,
        out_specs=vmem,
        name="pack",
    )(pair_recv, pair_src, pair_count, geometry, emission, occlusion)


def source_factors(geo, origin, rhs1, rhs2):
    centre, offsets, normal, area = frame(geo, origin)
    one = jnp.ones_like(area)
    zero = jnp.zeros_like(area)

    def put(ref, col, rows):
        hi, mid, lo = split3(jnp.concatenate(rows, 0))
        ref[:, col * TILE : (col + 1) * TILE] = jnp.concatenate(
            [hi, mid, lo, hi, mid, hi], 0
        ).astype(BF16)

    m2 = [-2.0 * x for x in centre]
    for q, b in enumerate(offsets):
        put(
            rhs1,
            q,
            [-2.0 * x for x in b]
            + m2
            + [dot3(b, b) + 2.0 * dot3(centre, b) + 0.25 * area, one],
        )
    put(rhs1, 4, list(normal) + [zero] * 3 + [-dot3(normal, centre), zero])
    weight = area * (1.0 / (16.0 * math.pi))
    for q, b in enumerate(offsets):
        put(
            rhs2,
            q,
            [(centre[c] + b[c]) * weight for c in range(3)] + [weight] + [zero] * 4,
        )
    for c in range(3):
        put(
            rhs2,
            4 + c,
            [zero] * 4 + [-one if c == k else zero for k in range(3)] + [centre[c]],
        )


def mm(a, b):
    return lax.dot_general(a, b, (((1,), (0,)), ((), ())), preferred_element_type=F32)


def mm_t(a, b):
    return lax.dot_general(a, b, (((1,), (1,)), ((), ())), preferred_element_type=F32)


def inverse_square(t):
    return 1.0 / (t * t)


def block_kernel(
    pay, geo_ref, left1, left2, refl, emis,
    blocks, out_b, out_sums, out_scale, out_code,
    rhs1, rhs2, word_s, acc_hi, acc_lo, buf, code_v, code, sem, code_sem,
):
    n_dev = pay.shape[0]
    own = refl.shape[1] // TILE
    origin = [geo_ref[c : c + 1, 0:1] for c in range(3)]
    lane = lax.broadcasted_iota(jnp.int32, (1, pay.shape[2]), 1)
    first = own * lax.axis_index("row")
    wide = lax.broadcasted_iota(jnp.int32, (n_dev, 128), 1)
    table = jnp.zeros((n_dev, 128), F32)
    rows = pay[:, ROW_CODE, :]
    for r in range(own):
        here = jnp.sum(jnp.where(lane == first + r, rows, 0.0), 1, keepdims=True)
        table = jnp.where(wide == r, here, table)
    code_v[...] = table.astype(jnp.int32)
    out_code[...] = table.astype(jnp.int32)
    to_scalar = pltpu.make_async_copy(code_v, code, code_sem)
    to_scalar.start()
    acc_hi[...] = jnp.zeros_like(acc_hi)
    acc_lo[...] = jnp.zeros_like(acc_lo)
    lane = lax.broadcasted_iota(jnp.int32, (1, TILE), 1)
    group_bit = jnp.left_shift(1, lane // (TILE // GROUPS))
    to_scalar.wait()

    def out_copy(slot, k):
        return pltpu.make_async_copy(buf.at[slot], blocks.at[k], sem.at[slot])

    def pair(k, done):
        r = k // n_dev
        j = k - r * n_dev
        value = code[j, r]

        @pl.when(value > 0)
        def _():
            slot = done & 1

            @pl.when(done >= 2)
            def _():
                out_copy(slot, k).wait()

            which = (value - 1) // 2
            lanes = pl.ds(pl.multiple_of(((value - 1) & 1) * TILE, TILE), TILE)
            geo = [pay[j, ROW_GEO + c : ROW_GEO + c + 1, lanes] for c in range(9)]
            source_factors(geo, origin, rhs1, rhs2)
            half = (ROW_GEO - ROW_OCC)
            side = (which >= half).astype(jnp.int32)
            word = pay[
                j,
                pl.ds(ROW_OCC + which - side * half, 1),
                pl.ds(pl.multiple_of(side * TILE, TILE), TILE),
            ].astype(jnp.int32)
            for c in range(2):
                part = jnp.broadcast_to(word[:, c * 128 : (c + 1) * 128], (128, 128))
                word_s[c * 128 : (c + 1) * 128, :] = jnp.transpose(part)

            def chunk(c, carry):
                rows = pl.ds(pl.multiple_of(c * CH, CH), CH)
                lhs2 = left2[pl.ds(pl.multiple_of(r * TILE + c * CH, CH), CH), :]
                lhs1 = left1[r * N_CH + c]
                d = [mm(lhs2, rhs2[:, (4 + x) * TILE : (5 + x) * TILE]) for x in range(3)]
                s = d[0] * d[0] + d[1] * d[1] + d[2] * d[2]
                facing = jnp.maximum(mm(lhs1, rhs1[:, 4 * TILE : 5 * TILE]), 0.0)
                total = None
                for q in range(4):
                    cols = slice(q * TILE, (q + 1) * TILE)
                    rest = mm(lhs1, rhs1[:, cols])
                    part = None
                    for p in range(4):
                        pr = slice(p * CH, (p + 1) * CH)
                        term = facing[pr] * inverse_square(s + rest[pr])
                        part = term if part is None else part + term
                    a = jnp.maximum(mm(lhs2, rhs2[:, cols]), 0.0) * part
                    total = a if total is None else total + a
                w = word_s[rows, :]
                w = jnp.concatenate([w, w], 1)
                total = jnp.where((w & group_bit) != 0, total, 0.0)
                hi, lo = split2(total)
                buf[slot, 0, rows, :] = hi
                buf[slot, 1, rows, :] = lo
                return carry

            lax.fori_loop(0, N_CH, chunk, 0, unroll=N_CH)
            out_copy(slot, k).start()
            x_hi, x_lo = split2(pay[j, 0:HOURS, lanes])
            ones = jnp.ones((16, TILE), BF16)
            acc_hi[r] += mm_t(jnp.concatenate([x_hi, x_lo, ones], 0), buf[slot, 0])
            acc_lo[r] += mm_t(jnp.concatenate([x_hi, ones], 0), buf[slot, 1])

        return done + (value > 0).astype(jnp.int32)

    done = lax.fori_loop(0, own * n_dev, pair, jnp.int32(0))
    for back in (1, 2):

        @pl.when(done >= back)
        def _():
            out_copy((done - back) & 1, 0).wait()

    for r in range(own):
        cols = slice(r * TILE, (r + 1) * TILE)
        irr = acc_hi[r, 0:16] + acc_hi[r, 16:32] + acc_lo[r, 0:16]
        sums = acc_hi[r, 32:33] + acc_lo[r, 16:17]
        scale = refl[:, cols] / jnp.maximum(sums, 1.0)
        out_sums[:, cols] = sums
        out_scale[:, cols] = scale
        out_b[:, cols] = emis[:, cols] + scale * irr


def view_blocks(pay, geometry, left1, left2, reflect, emission):
    vmem = pl.BlockSpec(memory_space=pltpu.VMEM)
    n_dev = pay.shape[0]
    width = emission.shape[1]
    own = width // TILE
    return pl.pallas_call(
        block_kernel,
        out_shape=(
            jax.ShapeDtypeStruct((own * n_dev, 2, TILE, TILE), BF16),
            jax.ShapeDtypeStruct((HOURS, width), F32),
            jax.ShapeDtypeStruct((1, width), F32),
            jax.ShapeDtypeStruct((1, width), F32),
            jax.ShapeDtypeStruct((n_dev, 128), jnp.int32),
        ),
        in_specs=[vmem] * 6,
        out_specs=(pl.BlockSpec(memory_space=pl.ANY), vmem, vmem, vmem, vmem),
        scratch_shapes=[
            pltpu.VMEM((SPLIT_K, 5 * TILE), BF16),
            pltpu.VMEM((SPLIT_K, 7 * TILE), BF16),
            pltpu.VMEM((TILE, 128), jnp.int32),
            pltpu.VMEM((own, 48, TILE), F32),
            pltpu.VMEM((own, 32, TILE), F32),
            pltpu.VMEM((2, 2, TILE, TILE), BF16),
            pltpu.VMEM((n_dev, 128), jnp.int32),
            pltpu.SMEM((n_dev, 128), jnp.int32),
            pltpu.SemaphoreType.DMA((2,)),
            pltpu.SemaphoreType.DMA,
        ],
        name="view_blocks",
    )(pay, geometry, left1, left2, reflect, emission)


def bounce_kernel(code, field, blocks, scale, emis, out, buf, sem, acc):
    n_dev = field.shape[0]
    acc[...] = jnp.zeros_like(acc)

    def copy(k):
        return pltpu.make_async_copy(blocks.at[k], buf.at[k], sem.at[k])

    def live(k):
        r = k // n_dev
        return code[k - r * n_dev, r]

    def begin(k, carry):
        @pl.when(live(k) > 0)
        def _():
            copy(k).start()

        return carry

    lax.fori_loop(0, 2 * n_dev, begin, 0)

    def pair(k, carry):
        value = live(k)

        @pl.when(value > 0)
        def _():
            r = k // n_dev
            j = k - r * n_dev
            src = (value - 1) & 1
            x_hi, x_lo = split2(field[j, :, pl.ds(pl.multiple_of(src * TILE, TILE), TILE)])
            both = jnp.concatenate([x_hi, x_lo], 0)
            copy(k).wait()
            first = mm_t(both, buf[k, 0])
            acc[r] += first[0:16] + first[16:32] + mm_t(x_hi, buf[k, 1])

        return carry

    lax.fori_loop(0, 2 * n_dev, pair, 0)
    for r in range(2):
        cols = slice(r * TILE, (r + 1) * TILE)
        out[:, cols] = emis[:, cols] + scale[:, cols] * acc[r]


def gather_rounds(x, n_dev):
    held = x[None]
    step = n_dev // 2
    while step:
        other = lax.ppermute(held, "row", [(i, i ^ step) for i in range(n_dev)])
        held = jnp.concatenate([held, other], 0)
        step //= 2
    return held


def on_device(geometry, emission, reflect, occlusion, pair_recv, pair_src, pair_count):
    width = geometry.shape[1]
    n_dev = lax.axis_size("row")
    payload = pack(geometry, emission, occlusion, pair_recv, pair_src, pair_count)
    left1, left2 = recv_factors(geometry)
    pay = gather_rounds(payload, n_dev)
    blocks, field, sums, scale, codes = view_blocks(
        pay, geometry, left1, left2, reflect[None], emission
    )
    fields = gather_rounds(field, n_dev)
    radiosity = pl.pallas_call(
        bounce_kernel,
        out_shape=jax.ShapeDtypeStruct((HOURS, width), F32),
        in_specs=[
            pl.BlockSpec(memory_space=pltpu.SMEM),
            pl.BlockSpec(memory_space=pltpu.VMEM),
            pl.BlockSpec(memory_space=pl.ANY),
            pl.BlockSpec(memory_space=pltpu.VMEM),
            pl.BlockSpec(memory_space=pltpu.VMEM),
        ],
        out_specs=pl.BlockSpec(memory_space=pltpu.VMEM),
        scratch_shapes=[
            pltpu.VMEM(blocks.shape, BF16),
            pltpu.SemaphoreType.DMA((blocks.shape[0],)),
            pltpu.VMEM((2, HOURS, TILE), F32),
        ],
        name="second_bounce",
    )(codes, fields, blocks, scale, emission)
    return (radiosity, sums[0])


def solution(mesh):
    placed = (
        P(None, ("grp", "row")),
        P(None, ("grp", "row")),
        P(("grp", "row")),
        P(("grp", "row"), None),
        P(("grp", "row")),
        P(("grp", "row")),
        P(("grp", "row")),
    )
    return jax.shard_map(
        on_device,
        mesh=mesh,
        in_specs=placed,
        out_specs=(P(None, ("grp", "row")), P(("grp", "row"))),
        check_vma=False,
    )
```

```python
import math

import jax
import jax.numpy as jnp
from jax import lax
from jax.experimental import pallas as pl
from jax.experimental.pallas import tpu as pltpu
from jax.sharding import PartitionSpec as P

TILE = 256
GROUPS = 16
HOURS = 16
CH = 32
N_CH = TILE // CH
SPLIT_K = 48
BF16 = jnp.bfloat16
F32 = jnp.float32

ROW_OCC = 16
ROW_GEO = 32
ROW_CODE = 41
ROWS = 48


def to_bf16(x):
    return x.astype(BF16).astype(F32)


def split3(x, narrow=to_bf16):
    hi = narrow(x)
    rest = x - hi
    mid = narrow(rest)
    return hi, mid, rest - mid


def split2(x):
    hi = x.astype(BF16)
    return hi, (x - hi.astype(F32)).astype(BF16)


def cross_of(u, v):
    return (
        u[1] * v[2] - u[2] * v[1],
        u[2] * v[0] - u[0] * v[2],
        u[0] * v[1] - u[1] * v[0],
    )


def dot3(a, b):
    return a[0] * b[0] + a[1] * b[1] + a[2] * b[2]


def frame(geo, origin):
    corner = [geo[c] - origin[c] for c in range(3)]
    u = [geo[3 + c] for c in range(3)]
    v = [geo[6 + c] for c in range(3)]
    centre = [corner[c] + 0.5 * (u[c] + v[c]) for c in range(3)]
    e1 = [0.25 * (u[c] + v[c]) for c in range(3)]
    e2 = [0.25 * (u[c] - v[c]) for c in range(3)]
    cross = cross_of(u, v)
    area = jnp.sqrt(dot3(cross, cross))
    normal = [cross[c] / area for c in range(3)]
    offsets = [e1, [-x for x in e1], e2, [-x for x in e2]]
    return centre, offsets, normal, area


def across(row):
    parts = [
        jnp.transpose(jnp.broadcast_to(row[:, c : c + 128], (128, 128)))
        for c in range(0, row.shape[1], 128)
    ]
    return jnp.concatenate(parts, 0)


def recv_kernel(geo_ref, left1, left2, centres):
    geo = [geo_ref[c : c + 1] for c in range(9)]
    origin = [geo[c][:, 0:1] for c in range(3)]
    centre, offsets, normal, _ = frame(geo, origin)
    one = jnp.ones_like(centre[0])
    zero = jnp.zeros_like(one)

    def columns(rows):
        hi, mid, lo = split3(jnp.concatenate(rows, 0))
        pad = [jnp.zeros_like(hi)] * ((128 - SPLIT_K) // 8)
        wide = jnp.concatenate([hi, hi, hi, mid, mid, lo] + pad, 0)
        return jnp.transpose(wide)[:, :SPLIT_K].astype(BF16)

    for p, a in enumerate(offsets):
        rows = [centre[c] + a[c] for c in range(3)] + list(a)
        rows += [one, dot3(a, a) + 2.0 * dot3(centre, a)]
        cols = columns(rows)
        for c in range(left1.shape[0]):
            left1[c, p * CH : (p + 1) * CH, :] = cols[c * CH : (c + 1) * CH]
    left2[...] = columns(list(normal) + [-dot3(normal, centre)] + [zero] * 4)
    for c in range(3):
        centres[c] = across(centre[c])


def recv_factors(geometry):
    width = geometry.shape[1]
    vmem = pl.BlockSpec(memory_space=pltpu.VMEM)
    return pl.pallas_call(
        recv_kernel,
        out_shape=(
            jax.ShapeDtypeStruct((width // CH, 4 * CH, SPLIT_K), BF16),
            jax.ShapeDtypeStruct((width, SPLIT_K), BF16),
            jax.ShapeDtypeStruct((3, width, 128), F32),
        ),
        in_specs=[vmem],
        out_specs=(vmem, vmem, vmem),
        cost_estimate=pl.CostEstimate(flops=200000, bytes_accessed=400000, transcendentals=1024),
        name="recv_factors",
    )(geometry)


def pack_kernel(recv, src, count, geo, emis, occ, out):
    slots = occ.shape[0]
    out[0:HOURS, :] = emis[...]
    words = occ[...].astype(F32)
    out[ROW_OCC : ROW_OCC + slots // 2, 0:TILE] = words[: slots // 2]
    out[ROW_OCC : ROW_OCC + slots // 2, TILE:] = words[slots // 2 :]
    out[ROW_GEO : ROW_GEO + 9, :] = geo[...]
    lane = lax.broadcasted_iota(jnp.int32, (1, out.shape[1]), 1)

    def slot(k, code):
        here = (lane == recv[k]) & (k < count[0])
        return jnp.where(here, 2 * k + src[k] + 1, code)

    code = lax.fori_loop(0, slots, slot, jnp.zeros_like(lane), unroll=8)
    out[ROW_CODE : ROW_CODE + 1, :] = code.astype(F32)
    out[ROW_CODE + 1 :, :] = jnp.zeros((ROWS - ROW_CODE - 1, out.shape[1]), F32)


def pack(geometry, emission, occlusion, pair_recv, pair_src, pair_count):
    vmem = pl.BlockSpec(memory_space=pltpu.VMEM)
    smem = pl.BlockSpec(memory_space=pltpu.SMEM)
    return pl.pallas_call(
        pack_kernel,
        out_shape=jax.ShapeDtypeStruct((ROWS, geometry.shape[1]), F32),
        in_specs=[smem] * 3 + [vmem] * 3,
        out_specs=vmem,
        name="pack",
    )(pair_recv, pair_src, pair_count, geometry, emission, occlusion)


def source_factors(geo, origin, rhs1, rhs2, middle):
    centre, offsets, normal, area = frame(geo, origin)
    one = jnp.ones_like(area)
    zero = jnp.zeros_like(area)

    def put(ref, col, rows):
        hi, mid, lo = split3(jnp.concatenate(rows, 0))
        ref[:, col * TILE : (col + 1) * TILE] = jnp.concatenate(
            [hi, mid, lo, hi, mid, hi], 0
        ).astype(BF16)

    m2 = [-2.0 * x for x in centre]
    for q, b in enumerate(offsets):
        put(
            rhs1,
            q,
            [-2.0 * x for x in b]
            + m2
            + [dot3(b, b) + 2.0 * dot3(centre, b) + 0.25 * area, one],
        )
    put(rhs1, 4, list(normal) + [zero] * 3 + [-dot3(normal, centre), zero])
    weight = area * (1.0 / (16.0 * math.pi))
    for q, b in enumerate(offsets):
        put(
            rhs2,
            q,
            [(centre[c] + b[c]) * weight for c in range(3)] + [weight] + [zero] * 4,
        )
    for c in range(3):
        middle[c : c + 1, :] = centre[c]


def mm(a, b):
    return lax.dot_general(a, b, (((1,), (0,)), ((), ())), preferred_element_type=F32)


def mm_t(a, b):
    return lax.dot_general(a, b, (((1,), (1,)), ((), ())), preferred_element_type=F32)


def inverse_square(t):
    return 1.0 / (t * t)


def block_kernel(
    pay, geo_ref, left1, left2, centres, refl, emis,
    blocks, out_b, out_sums, out_scale, order,
    rhs1, rhs2, middle, next1, next2, next_middle, word_s, acc_hi, acc_lo,
    code_v, code, code_sem,
):
    n_dev = pay.shape[0]
    own = refl.shape[1] // TILE
    pairs = own * n_dev
    origin = [geo_ref[c : c + 1, 0:1] for c in range(3)]
    lane = lax.broadcasted_iota(jnp.int32, (1, pay.shape[2]), 1)
    first = own * lax.axis_index("row")
    wide = lax.broadcasted_iota(jnp.int32, (n_dev, 128), 1)
    table = jnp.zeros((n_dev, 128), F32)
    rows = pay[:, ROW_CODE, :]
    for r in range(own):
        here = jnp.sum(jnp.where(lane == first + r, rows, 0.0), 1, keepdims=True)
        table = jnp.where(wide == r, here, table)
    code_v[...] = table.astype(jnp.int32)
    to_scalar = pltpu.make_async_copy(code_v, code, code_sem)
    to_scalar.start()
    acc_hi[...] = jnp.zeros_like(acc_hi)
    acc_lo[...] = jnp.zeros_like(acc_lo)
    lane = lax.broadcasted_iota(jnp.int32, (1, TILE), 1)
    group_bit = jnp.left_shift(1, lane // (TILE // GROUPS))
    to_scalar.wait()

    half = ROW_GEO - ROW_OCC
    order[0] = 0

    def listed(k, count):
        r = k // n_dev
        value = code[k - r * n_dev, r]
        order[1 + count] = jnp.maximum(value - 1, 0) * pairs + k
        return count + (value > 0).astype(jnp.int32)

    n = lax.fori_loop(0, pairs, listed, jnp.int32(0))
    order[0] = n
    order[1 + n] = 0

    def where_is(i):
        entry = order[1 + i]
        value = entry // pairs
        k = entry - value * pairs
        r = k // n_dev
        return r, k - r * n_dev, value

    def source_lanes(value):
        return pl.ds(pl.multiple_of((value & 1) * TILE, TILE), TILE)

    def prepare(i):
        _, j, value = where_is(i)
        lanes = source_lanes(value)
        geo = [pay[j, ROW_GEO + c : ROW_GEO + c + 1, lanes] for c in range(9)]
        source_factors(geo, origin, next1, next2, next_middle)

    def deposit(i):
        r, j, value = where_is(i)
        x_hi, x_lo = split2(pay[j, 0:HOURS, source_lanes(value)])
        ones = jnp.ones((16, TILE), BF16)
        acc_hi[r] += mm_t(jnp.concatenate([x_hi, x_lo, ones], 0), blocks[i, 0])
        acc_lo[r] += mm_t(jnp.concatenate([x_hi, ones], 0), blocks[i, 1])

    def pair(i, carry):
        r, j, value = where_is(i)
        rhs1[...] = next1[...]
        rhs2[...] = next2[...]
        middle[...] = next_middle[...]
        which = value // 2
        side = (which >= half).astype(jnp.int32)
        word = pay[
            j,
            pl.ds(ROW_OCC + which - side * half, 1),
            pl.ds(pl.multiple_of(side * TILE, TILE), TILE),
        ].astype(jnp.int32)
        word_s[...] = across(word)
        prepare(i + 1)
        for c in range(N_CH):
            rows = slice(c * CH, (c + 1) * CH)
            own_rows = pl.ds(pl.multiple_of(r * TILE + c * CH, CH), CH)
            lhs2 = left2[own_rows, :]
            lhs1 = left1[r * N_CH + c]
            s = None
            for x in range(3):
                mine = centres[x, own_rows, :]
                d = middle[x : x + 1, :] - jnp.concatenate([mine, mine], 1)
                s = d * d if s is None else s + d * d
            facing = jnp.maximum(mm(lhs1, rhs1[:, 4 * TILE : 5 * TILE]), 0.0)
            total = None
            for q in range(4):
                cols = slice(q * TILE, (q + 1) * TILE)
                rest = mm(lhs1, rhs1[:, cols])
                part = None
                for p in range(4):
                    pr = slice(p * CH, (p + 1) * CH)
                    term = facing[pr] * inverse_square(s + rest[pr])
                    part = term if part is None else part + term
                a = jnp.maximum(mm(lhs2, rhs2[:, cols]), 0.0) * part
                total = a if total is None else total + a
            w = word_s[rows, :]
            w = jnp.concatenate([w, w], 1)
            total = jnp.where((w & group_bit) != 0, total, 0.0)
            hi, lo = split2(total)
            blocks[i, 0, rows, :] = hi
            blocks[i, 1, rows, :] = lo
        deposit(i)
        return carry

    prepare(0)
    lax.fori_loop(0, n, pair, 0)

    for r in range(own):
        cols = slice(r * TILE, (r + 1) * TILE)
        irr = acc_hi[r, 0:16] + acc_hi[r, 16:32] + acc_lo[r, 0:16]
        sums = acc_hi[r, 32:33] + acc_lo[r, 16:17]
        scale = refl[:, cols] / jnp.maximum(sums, 1.0)
        out_sums[:, cols] = sums
        out_scale[:, cols] = scale
        out_b[:, cols] = emis[:, cols] + scale * irr


def view_blocks(pay, geometry, left1, left2, centres, reflect, emission):
    vmem = pl.BlockSpec(memory_space=pltpu.VMEM)
    n_dev = pay.shape[0]
    width = emission.shape[1]
    own = width // TILE
    pairs = own * n_dev
    return pl.pallas_call(
        block_kernel,
        out_shape=(
            jax.ShapeDtypeStruct((pairs, 2, TILE, TILE), BF16),
            jax.ShapeDtypeStruct((HOURS, width), F32),
            jax.ShapeDtypeStruct((1, width), F32),
            jax.ShapeDtypeStruct((1, width), F32),
            jax.ShapeDtypeStruct((2 * pairs,), jnp.int32),
        ),
        in_specs=[vmem] * 7,
        out_specs=(vmem, vmem, vmem, vmem, pl.BlockSpec(memory_space=pltpu.SMEM)),
        scratch_shapes=[
            pltpu.VMEM((SPLIT_K, 5 * TILE), BF16),
            pltpu.VMEM((SPLIT_K, 4 * TILE), BF16),
            pltpu.VMEM((8, TILE), F32),
            pltpu.VMEM((SPLIT_K, 5 * TILE), BF16),
            pltpu.VMEM((SPLIT_K, 4 * TILE), BF16),
            pltpu.VMEM((8, TILE), F32),
            pltpu.VMEM((TILE, 128), jnp.int32),
            pltpu.VMEM((own, 48, TILE), F32),
            pltpu.VMEM((own, 32, TILE), F32),
            pltpu.VMEM((n_dev, 128), jnp.int32),
            pltpu.SMEM((n_dev, 128), jnp.int32),
            pltpu.SemaphoreType.DMA,
        ],
        compiler_params=pltpu.CompilerParams(vmem_limit_bytes=12 << 20),
        name="view_blocks",
    )(pay, geometry, left1, left2, centres, reflect, emission)


def bounce_kernel(order, field, blocks, scale, emis, out, acc):
    n_dev = field.shape[0]
    own = out.shape[1] // TILE
    pairs = own * n_dev
    n = order[0]
    acc[...] = jnp.zeros_like(acc)

    def some(step, carry):
        for b in range(4):
            i = 4 * step + b
            live = i < n
            entry = jnp.where(live, order[1 + i], 0)
            value = entry // pairs
            k = entry - value * pairs
            r = k // n_dev
            j = k - r * n_dev
            at = jnp.minimum(i, pairs - 1)
            lanes = pl.ds(pl.multiple_of((value & 1) * TILE, TILE), TILE)
            x_hi, x_lo = split2(field[j, :, lanes])
            both = mm_t(jnp.concatenate([x_hi, x_lo], 0), blocks[at, 0])
            got = both[0:16] + both[16:32] + mm_t(x_hi, blocks[at, 1])
            acc[r] += jnp.where(live, got, 0.0)
        return carry

    lax.fori_loop(0, (n + 3) // 4, some, 0)
    for r in range(own):
        cols = slice(r * TILE, (r + 1) * TILE)
        out[:, cols] = emis[:, cols] + scale[:, cols] * acc[r]


def second_bounce(order, field, blocks, scale, emission):
    vmem = pl.BlockSpec(memory_space=pltpu.VMEM)
    own = emission.shape[1] // TILE
    return pl.pallas_call(
        bounce_kernel,
        out_shape=jax.ShapeDtypeStruct(emission.shape, F32),
        in_specs=[pl.BlockSpec(memory_space=pltpu.SMEM)] + [vmem] * 4,
        out_specs=vmem,
        scratch_shapes=[pltpu.VMEM((own, HOURS, TILE), F32)],
        compiler_params=pltpu.CompilerParams(vmem_limit_bytes=12 << 20),
        name="second_bounce",
    )(order, field, blocks, scale, emission)


def gather_rounds(x, n_dev):
    held = x[None]
    step = n_dev // 2
    while step:
        other = lax.ppermute(held, "row", [(i, i ^ step) for i in range(n_dev)])
        held = jnp.concatenate([held, other], 0)
        step //= 2
    return held


def on_device(geometry, emission, reflect, occlusion, pair_recv, pair_src, pair_count):
    width = geometry.shape[1]
    n_dev = lax.axis_size("row")
    payload = pack(geometry, emission, occlusion, pair_recv, pair_src, pair_count)
    left1, left2, centres = recv_factors(geometry)
    pay = gather_rounds(payload, n_dev)
    blocks, field, sums, scale, order = view_blocks(
        pay, geometry, left1, left2, centres, reflect[None], emission
    )
    fields = gather_rounds(field, n_dev)
    radiosity = second_bounce(order, fields, blocks, scale, emission)
    return (radiosity, sums[0])


def solution(mesh):
    placed = (
        P(None, ("grp", "row")),
        P(None, ("grp", "row")),
        P(("grp", "row")),
        P(("grp", "row"), None),
        P(("grp", "row")),
        P(("grp", "row")),
        P(("grp", "row")),
    )
    return jax.shard_map(
        on_device,
        mesh=mesh,
        in_specs=placed,
        out_specs=(P(None, ("grp", "row")), P(("grp", "row"))),
        check_vma=False,
    )
```

```python
import math

import jax
import jax.numpy as jnp
from jax import lax
from jax.experimental import pallas as pl
from jax.experimental.pallas import tpu as pltpu
from jax.sharding import PartitionSpec as P

TILE = 256
GROUPS = 16
HOURS = 16
CH = 32
N_CH = TILE // CH
SPLIT_K = 48
BF16 = jnp.bfloat16
F32 = jnp.float32

LANES = 128
SHARED = 10


def to_bf16(x):
    return x.astype(BF16).astype(F32)


def split3(x, narrow=to_bf16):
    hi = narrow(x)
    rest = x - hi
    mid = narrow(rest)
    return hi, mid, rest - mid


def split2(x):
    hi = x.astype(BF16)
    return hi, (x - hi.astype(F32)).astype(BF16)


def cross_of(u, v):
    return (
        u[1] * v[2] - u[2] * v[1],
        u[2] * v[0] - u[0] * v[2],
        u[0] * v[1] - u[1] * v[0],
    )


def dot3(a, b):
    return a[0] * b[0] + a[1] * b[1] + a[2] * b[2]


def frame(geo, origin):
    corner = [geo[c] - origin[c] for c in range(3)]
    u = [geo[3 + c] for c in range(3)]
    v = [geo[6 + c] for c in range(3)]
    centre = [corner[c] + 0.5 * (u[c] + v[c]) for c in range(3)]
    e1 = [0.25 * (u[c] + v[c]) for c in range(3)]
    e2 = [0.25 * (u[c] - v[c]) for c in range(3)]
    cross = cross_of(u, v)
    area = jnp.sqrt(dot3(cross, cross))
    normal = [cross[c] / area for c in range(3)]
    offsets = [e1, [-x for x in e1], e2, [-x for x in e2]]
    return centre, offsets, normal, area


def across(row):
    parts = [
        jnp.transpose(jnp.broadcast_to(row[:, c : c + 128], (128, 128)))
        for c in range(0, row.shape[1], 128)
    ]
    return jnp.concatenate(parts, 0)


def recv_kernel(geo_ref, refl, left1, left2, centres, refl_out):
    geo = [geo_ref[c : c + 1] for c in range(9)]
    origin = [geo[c][:, 0:1] for c in range(3)]
    centre, offsets, normal, _ = frame(geo, origin)
    one = jnp.ones_like(centre[0])
    zero = jnp.zeros_like(one)

    def columns(rows):
        hi, mid, lo = split3(jnp.concatenate(rows, 0))
        pad = [jnp.zeros_like(hi)] * ((128 - SPLIT_K) // 8)
        wide = jnp.concatenate([hi, hi, hi, mid, mid, lo] + pad, 0)
        return jnp.transpose(wide)[:, :SPLIT_K].astype(BF16)

    for p, a in enumerate(offsets):
        rows = [centre[c] + a[c] for c in range(3)] + list(a)
        rows += [one, dot3(a, a) + 2.0 * dot3(centre, a)]
        cols = columns(rows)
        for c in range(left1.shape[0]):
            left1[c, p * CH : (p + 1) * CH, :] = cols[c * CH : (c + 1) * CH]
    left2[...] = columns(list(normal) + [-dot3(normal, centre)] + [zero] * 4)
    for c in range(3):
        centres[c] = across(centre[c])
    refl_out[...] = refl[...]


def recv_factors(geometry, reflect):
    width = geometry.shape[1]
    vmem = pl.BlockSpec(memory_space=pltpu.VMEM)
    return pl.pallas_call(
        recv_kernel,
        out_shape=(
            jax.ShapeDtypeStruct((width // CH, 4 * CH, SPLIT_K), BF16),
            jax.ShapeDtypeStruct((width, SPLIT_K), BF16),
            jax.ShapeDtypeStruct((3, width, 128), F32),
            jax.ShapeDtypeStruct((1, width), F32),
        ),
        in_specs=[vmem] * 2,
        out_specs=(vmem,) * 4,
        cost_estimate=pl.CostEstimate(flops=200000, bytes_accessed=1600000, transcendentals=1024),
        compiler_params=pltpu.CompilerParams(vmem_limit_bytes=4 << 20),
        name="recv_factors",
    )(geometry, reflect)


def pack_kernel(
    count, recv_h, src_h, geo_h, emis_h, occ_h, shared, words,
    recv, src, geo, emis, occ, sem,
):
    chunks = emis.shape[1] // LANES
    own = emis.shape[1] // TILE
    me = lax.axis_index("row")
    copies = [
        pltpu.make_async_copy(a, b, sem.at[i])
        for i, (a, b) in enumerate(
            ((recv_h, recv), (src_h, src), (geo_h, geo), (emis_h, emis), (occ_h, occ))
        )
    ]
    for copy in copies:
        copy.start()
    words[...] = jnp.zeros_like(words)
    for copy in copies:
        copy.wait()
    for c in range(chunks):
        lanes = slice(c * LANES, (c + 1) * LANES)
        shared[c * HOURS : (c + 1) * HOURS, :] = emis[:, lanes]
        start = chunks * HOURS + c * SHARED
        shared[start : start + 9, :] = geo[:, lanes]
        shared[start + 9 : start + 10, :] = jnp.zeros((1, LANES), F32)
    lane = lax.broadcasted_iota(jnp.int32, (1, LANES), 1)

    def slot(k, code):
        tile = recv[k]
        owner = tile // own
        row = 2 * (tile - owner * own)
        line = occ[pl.ds(k, 1), :].astype(F32)
        for c in range(2):
            words[owner ^ me, pl.ds(row + c, 1), :] = line[:, c * LANES : (c + 1) * LANES]
        return jnp.where(lane == tile, 1 + src[k], code)

    code = lax.fori_loop(0, count[0], slot, jnp.zeros_like(lane))
    start = chunks * HOURS + 9
    shared[start : start + 1, :] = code.astype(F32)


def pack(geometry, emission, occlusion, pair_recv, pair_src, pair_count):
    vmem = pl.BlockSpec(memory_space=pltpu.VMEM)
    smem = pl.BlockSpec(memory_space=pltpu.SMEM)
    hbm = pl.BlockSpec(memory_space=pltpu.HBM)
    width = geometry.shape[1]
    n_dev = lax.axis_size("row")
    large = [
        pltpu.with_memory_space_constraint(x, pltpu.HBM)
        for x in (pair_recv, pair_src, geometry, emission, occlusion)
    ]
    return pl.pallas_call(
        pack_kernel,
        out_shape=(
            jax.ShapeDtypeStruct((width // LANES * (HOURS + SHARED), LANES), F32),
            jax.ShapeDtypeStruct((n_dev, width // LANES, LANES), F32),
        ),
        in_specs=[smem] + [hbm] * 5,
        out_specs=(vmem, vmem),
        scratch_shapes=[
            pltpu.SMEM(pair_recv.shape, jnp.int32),
            pltpu.SMEM(pair_src.shape, jnp.int32),
            pltpu.VMEM(geometry.shape, F32),
            pltpu.VMEM(emission.shape, F32),
            pltpu.VMEM(occlusion.shape, jnp.int32),
            pltpu.SemaphoreType.DMA((5,)),
        ],
        compiler_params=pltpu.CompilerParams(vmem_limit_bytes=4 << 20),
        name="pack",
    )(pair_count, *large)


def source_factors(geo, origin, rhs1, rhs2, middle):
    centre, offsets, normal, area = frame(geo, origin)
    one = jnp.ones_like(area)
    zero = jnp.zeros_like(area)

    def put(ref, col, rows):
        hi, mid, lo = split3(jnp.concatenate(rows, 0))
        ref[:, col * TILE : (col + 1) * TILE] = jnp.concatenate(
            [hi, mid, lo, hi, mid, hi], 0
        ).astype(BF16)

    m2 = [-2.0 * x for x in centre]
    for q, b in enumerate(offsets):
        put(
            rhs1,
            q,
            [-2.0 * x for x in b]
            + m2
            + [dot3(b, b) + 2.0 * dot3(centre, b) + 0.25 * area, one],
        )
    put(rhs1, 4, list(normal) + [zero] * 3 + [-dot3(normal, centre), zero])
    weight = area * (1.0 / (16.0 * math.pi))
    for q, b in enumerate(offsets):
        put(
            rhs2,
            q,
            [(centre[c] + b[c]) * weight for c in range(3)] + [weight] + [zero] * 4,
        )
    for c in range(3):
        middle[c : c + 1, :] = centre[c]


def mm(a, b):
    return lax.dot_general(a, b, (((1,), (0,)), ((), ())), preferred_element_type=F32)


def mm_t(a, b):
    return lax.dot_general(a, b, (((1,), (1,)), ((), ())), preferred_element_type=F32)


def inverse_square(t):
    return 1.0 / (t * t)


def block_kernel(
    pay, words, left1, left2, centres, refl,
    blocks, out_b, out_sums, out_scale, order,
    rhs1, rhs2, middle, next1, next2, next_middle, word_s, acc_hi, acc_lo,
    code_v, code, code_sem,
):
    n_dev = pay.shape[0]
    own = refl.shape[1] // TILE
    pairs = own * n_dev
    chunks = refl.shape[1] // LANES
    geo_row = chunks * HOURS
    origin = [pay[0, geo_row + c : geo_row + c + 1, 0:1] for c in range(3)]
    lane = lax.broadcasted_iota(jnp.int32, (1, LANES), 1)
    first = own * lax.axis_index("row")
    wide = lax.broadcasted_iota(jnp.int32, (n_dev, LANES), 1)
    table = jnp.zeros((n_dev, LANES), F32)
    rows = pay[:, geo_row + 9, :]
    for r in range(own):
        here = jnp.sum(jnp.where(lane == first + r, rows, 0.0), 1, keepdims=True)
        table = jnp.where(wide == r, here, table)
    code_v[...] = table.astype(jnp.int32)
    to_scalar = pltpu.make_async_copy(code_v, code, code_sem)
    to_scalar.start()
    acc_hi[...] = jnp.zeros_like(acc_hi)
    acc_lo[...] = jnp.zeros_like(acc_lo)
    lane = lax.broadcasted_iota(jnp.int32, (1, TILE), 1)
    group_bit = jnp.left_shift(1, lane // (TILE // GROUPS))
    to_scalar.wait()

    order[0] = 0

    def listed(k, count):
        r = k // n_dev
        value = code[k - r * n_dev, r]
        order[1 + count] = jnp.maximum(value - 1, 0) * pairs + k
        return count + (value > 0).astype(jnp.int32)

    n = lax.fori_loop(0, pairs, listed, jnp.int32(0))
    order[0] = n
    order[1 + n] = 0

    def where_is(i):
        entry = order[1 + i]
        value = entry // pairs
        k = entry - value * pairs
        r = k // n_dev
        return r, k - r * n_dev, value

    def prepare(i):
        _, j, source = where_is(i)
        at = geo_row + 2 * SHARED * source
        geo = [
            jnp.concatenate(
                [pay[j, pl.ds(at + c, 1), :], pay[j, pl.ds(at + SHARED + c, 1), :]], 1
            )
            for c in range(9)
        ]
        source_factors(geo, origin, next1, next2, next_middle)

    def deposit(i):
        r, j, source = where_is(i)
        at = pl.multiple_of(2 * HOURS * source, HOURS)
        x = jnp.concatenate(
            [pay[j, pl.ds(at, HOURS), :], pay[j, pl.ds(at + HOURS, HOURS), :]], 1
        )
        x_hi, x_lo = split2(x)
        ones = jnp.ones((16, TILE), BF16)
        acc_hi[r] += mm_t(jnp.concatenate([x_hi, x_lo, ones], 0), blocks[i, 0])
        acc_lo[r] += mm_t(jnp.concatenate([x_hi, ones], 0), blocks[i, 1])

    def pair(i, carry):
        r, j, _ = where_is(i)
        rhs1[...] = next1[...]
        rhs2[...] = next2[...]
        middle[...] = next_middle[...]
        for c in range(2):
            word_s[c * LANES : (c + 1) * LANES, :] = across(
                words[j, pl.ds(2 * r + c, 1), :].astype(jnp.int32)
            )
        prepare(i + 1)
        for c in range(N_CH):
            rows = slice(c * CH, (c + 1) * CH)
            own_rows = pl.ds(pl.multiple_of(r * TILE + c * CH, CH), CH)
            lhs2 = left2[own_rows, :]
            lhs1 = left1[r * N_CH + c]
            s = None
            for x in range(3):
                mine = centres[x, own_rows, :]
                d = middle[x : x + 1, :] - jnp.concatenate([mine, mine], 1)
                s = d * d if s is None else s + d * d
            facing = jnp.maximum(mm(lhs1, rhs1[:, 4 * TILE : 5 * TILE]), 0.0)
            total = None
            for q in range(4):
                cols = slice(q * TILE, (q + 1) * TILE)
                rest = mm(lhs1, rhs1[:, cols])
                part = None
                for p in range(4):
                    pr = slice(p * CH, (p + 1) * CH)
                    term = facing[pr] * inverse_square(s + rest[pr])
                    part = term if part is None else part + term
                a = jnp.maximum(mm(lhs2, rhs2[:, cols]), 0.0) * part
                total = a if total is None else total + a
            w = word_s[rows, :]
            w = jnp.concatenate([w, w], 1)
            total = jnp.where((w & group_bit) != 0, total, 0.0)
            hi, lo = split2(total)
            blocks[i, 0, rows, :] = hi
            blocks[i, 1, rows, :] = lo
        deposit(i)
        return carry

    prepare(0)
    lax.fori_loop(0, n, pair, 0)

    for r in range(own):
        cols = slice(r * TILE, (r + 1) * TILE)
        irr = acc_hi[r, 0:16] + acc_hi[r, 16:32] + acc_lo[r, 0:16]
        sums = acc_hi[r, 32:33] + acc_lo[r, 16:17]
        scale = refl[:, cols] / jnp.maximum(sums, 1.0)
        out_sums[:, cols] = sums
        out_scale[:, cols] = scale
        emis = [pay[0, c * HOURS : (c + 1) * HOURS, :] for c in (2 * r, 2 * r + 1)]
        out_b[:, cols] = jnp.concatenate(emis, 1) + scale * irr


def view_blocks(pay, words, left1, left2, centres, reflect):
    vmem = pl.BlockSpec(memory_space=pltpu.VMEM)
    n_dev = pay.shape[0]
    width = reflect.shape[1]
    own = width // TILE
    pairs = own * n_dev
    return pl.pallas_call(
        block_kernel,
        out_shape=(
            jax.ShapeDtypeStruct((pairs, 2, TILE, TILE), BF16),
            jax.ShapeDtypeStruct((HOURS, width), F32),
            jax.ShapeDtypeStruct((1, width), F32),
            jax.ShapeDtypeStruct((1, width), F32),
            jax.ShapeDtypeStruct((2 * pairs,), jnp.int32),
        ),
        in_specs=[vmem] * 6,
        out_specs=(vmem, vmem, vmem, vmem, pl.BlockSpec(memory_space=pltpu.SMEM)),
        scratch_shapes=[
            pltpu.VMEM((SPLIT_K, 5 * TILE), BF16),
            pltpu.VMEM((SPLIT_K, 4 * TILE), BF16),
            pltpu.VMEM((8, TILE), F32),
            pltpu.VMEM((SPLIT_K, 5 * TILE), BF16),
            pltpu.VMEM((SPLIT_K, 4 * TILE), BF16),
            pltpu.VMEM((8, TILE), F32),
            pltpu.VMEM((TILE, 128), jnp.int32),
            pltpu.VMEM((own, 48, TILE), F32),
            pltpu.VMEM((own, 32, TILE), F32),
            pltpu.VMEM((n_dev, 128), jnp.int32),
            pltpu.SMEM((n_dev, 128), jnp.int32),
            pltpu.SemaphoreType.DMA,
        ],
        compiler_params=pltpu.CompilerParams(vmem_limit_bytes=12 << 20),
        name="view_blocks",
    )(pay, words, left1, left2, centres, reflect)


def bounce_kernel(order, field, blocks, scale, emis, out, acc):
    n_dev = field.shape[0]
    own = out.shape[1] // TILE
    pairs = own * n_dev
    n = order[0]
    acc[...] = jnp.zeros_like(acc)

    def some(step, carry):
        for b in range(4):
            i = 4 * step + b
            live = i < n
            entry = jnp.where(live, order[1 + i], 0)
            value = entry // pairs
            k = entry - value * pairs
            r = k // n_dev
            j = k - r * n_dev
            at = jnp.minimum(i, pairs - 1)
            lanes = pl.ds(pl.multiple_of(value * TILE, TILE), TILE)
            x_hi, x_lo = split2(field[j, :, lanes])
            both = mm_t(jnp.concatenate([x_hi, x_lo], 0), blocks[at, 0])
            got = both[0:16] + both[16:32] + mm_t(x_hi, blocks[at, 1])
            acc[r] += jnp.where(live, got, 0.0)
        return carry

    lax.fori_loop(0, (n + 3) // 4, some, 0)
    for r in range(own):
        cols = slice(r * TILE, (r + 1) * TILE)
        out[:, cols] = emis[:, cols] + scale[:, cols] * acc[r]


def second_bounce(order, field, blocks, scale, emission):
    vmem = pl.BlockSpec(memory_space=pltpu.VMEM)
    own = emission.shape[1] // TILE
    return pl.pallas_call(
        bounce_kernel,
        out_shape=jax.ShapeDtypeStruct(emission.shape, F32),
        in_specs=[pl.BlockSpec(memory_space=pltpu.SMEM)] + [vmem] * 4,
        out_specs=vmem,
        scratch_shapes=[pltpu.VMEM((own, HOURS, TILE), F32)],
        compiler_params=pltpu.CompilerParams(vmem_limit_bytes=12 << 20),
        name="second_bounce",
    )(order, field, blocks, scale, emission)


def gather_rounds(x, n_dev):
    held = x[None]
    step = n_dev // 2
    while step:
        other = lax.ppermute(held, "row", [(i, i ^ step) for i in range(n_dev)])
        held = jnp.concatenate([held, other], 0)
        step //= 2
    return held


def gather_and_deal(shared, words, n_dev, beside):
    held, words = shared[None], words[None]
    step = n_dev // 2
    while step:
        lines = held.shape[0] * held.shape[1]
        keep, send = words[:, :step], words[:, step:]
        message = jnp.concatenate([held.reshape(-1, LANES), send.reshape(-1, LANES)], 0)
        other = lax.ppermute(message, "row", [(i, i ^ step) for i in range(n_dev)])
        if step == 2:
            other, beside = lax.optimization_barrier((other, beside))
        held = jnp.concatenate([held, other[:lines].reshape(held.shape)], 0)
        words = jnp.concatenate([keep, other[lines:].reshape(send.shape)], 0)
        step //= 2
    return held, words[:, 0], beside


def on_device(geometry, emission, reflect, occlusion, pair_recv, pair_src, pair_count):
    n_dev = lax.axis_size("row")
    shared, words = pack(geometry, emission, occlusion, pair_recv, pair_src, pair_count)
    left = recv_factors(geometry, reflect[None])
    pay, words, left = gather_and_deal(shared, words, n_dev, left)
    blocks, field, sums, scale, order = view_blocks(pay, words, *left)
    fields = gather_rounds(field, n_dev)
    radiosity = second_bounce(order, fields, blocks, scale, emission)
    return (radiosity, sums[0])


def solution(mesh):
    placed = (
        P(None, ("grp", "row")),
        P(None, ("grp", "row")),
        P(("grp", "row")),
        P(("grp", "row"), None),
        P(("grp", "row")),
        P(("grp", "row")),
        P(("grp", "row")),
    )
    return jax.shard_map(
        on_device,
        mesh=mesh,
        in_specs=placed,
        out_specs=(P(None, ("grp", "row")), P(("grp", "row"))),
        check_vma=False,
    )
```

```python
import functools
import math

import jax
import jax.numpy as jnp
from jax import lax
from jax.experimental import pallas as pl
from jax.experimental.pallas import tpu as pltpu
from jax.sharding import PartitionSpec as P

TILE = 256
GROUPS = 16
HOURS = 16
CH = 32
N_CH = TILE // CH
SPLIT_K = 48
BF16 = jnp.bfloat16
F32 = jnp.float32

LANES = 128
SHARED = 10
AREA_MIN = 0.2
NEAR = 4e-4


def to_bf16(x):
    return x.astype(BF16).astype(F32)


def split3(x, narrow=to_bf16):
    hi = narrow(x)
    rest = x - hi
    mid = narrow(rest)
    return hi, mid, rest - mid


def split2(x):
    hi = x.astype(BF16)
    return hi, (x - hi.astype(F32)).astype(BF16)


def cross_of(u, v):
    return (
        u[1] * v[2] - u[2] * v[1],
        u[2] * v[0] - u[0] * v[2],
        u[0] * v[1] - u[1] * v[0],
    )


def dot3(a, b):
    return a[0] * b[0] + a[1] * b[1] + a[2] * b[2]


def frame(geo, origin):
    corner = [geo[c] - origin[c] for c in range(3)]
    u = [geo[3 + c] for c in range(3)]
    v = [geo[6 + c] for c in range(3)]
    centre = [corner[c] + 0.5 * (u[c] + v[c]) for c in range(3)]
    e1 = [0.25 * (u[c] + v[c]) for c in range(3)]
    e2 = [0.25 * (u[c] - v[c]) for c in range(3)]
    cross = cross_of(u, v)
    area = jnp.sqrt(dot3(cross, cross))
    normal = [cross[c] / area for c in range(3)]
    offsets = [e1, [-x for x in e1], e2, [-x for x in e2]]
    return centre, offsets, normal, area


def across(row):
    parts = [
        jnp.transpose(jnp.broadcast_to(row[:, c : c + 128], (128, 128)))
        for c in range(0, row.shape[1], 128)
    ]
    return jnp.concatenate(parts, 0)


def recv_kernel(geo_ref, refl, left0, left1, left2, centres, refl_out, middle_out):
    geo = [geo_ref[c : c + 1] for c in range(9)]
    origin = [jnp.mean(geo[c], 1, keepdims=True) for c in range(3)]
    middle_out[...] = jnp.concatenate(
        [jnp.broadcast_to(x, (1, LANES)) for x in origin] + [jnp.zeros((5, LANES), F32)], 0
    )
    centre, offsets, normal, _ = frame(geo, origin)
    one = jnp.ones_like(centre[0])
    zero = jnp.zeros_like(one)

    def columns(rows):
        hi, mid, lo = split3(jnp.concatenate(rows, 0))
        pad = [jnp.zeros_like(hi)] * ((128 - SPLIT_K) // 8)
        wide = jnp.concatenate([hi, hi, hi, mid, mid, lo] + pad, 0)
        return jnp.transpose(wide)[:, :SPLIT_K].astype(BF16)

    for p, a in enumerate(offsets):
        point = [centre[c] + a[c] for c in range(3)]
        cols0 = columns(point + [dot3(point, point), one] + [zero] * 3)
        cols1 = columns(point + list(a) + [one, dot3(a, a) + 2.0 * dot3(centre, a)])
        for c in range(left1.shape[0]):
            rows = slice(c * CH, (c + 1) * CH)
            left0[c, p * CH : (p + 1) * CH, :] = cols0[rows]
            left1[c, p * CH : (p + 1) * CH, :] = cols1[rows]
    left2[...] = columns(list(normal) + [-dot3(normal, centre)] + [zero] * 4)
    for c in range(3):
        centres[c] = across(centre[c])
    refl_out[...] = refl[...]


def recv_factors(geometry, reflect):
    width = geometry.shape[1]
    vmem = pl.BlockSpec(memory_space=pltpu.VMEM)
    return pl.pallas_call(
        recv_kernel,
        out_shape=(
            jax.ShapeDtypeStruct((width // CH, 4 * CH, SPLIT_K), BF16),
            jax.ShapeDtypeStruct((width // CH, 4 * CH, SPLIT_K), BF16),
            jax.ShapeDtypeStruct((width, SPLIT_K), BF16),
            jax.ShapeDtypeStruct((3, width, 128), F32),
            jax.ShapeDtypeStruct((1, width), F32),
            jax.ShapeDtypeStruct((8, LANES), F32),
        ),
        in_specs=[vmem] * 2,
        out_specs=(vmem,) * 6,
        cost_estimate=pl.CostEstimate(flops=200000, bytes_accessed=1600000, transcendentals=1024),
        compiler_params=pltpu.CompilerParams(vmem_limit_bytes=4 << 20),
        name="recv_factors",
    )(geometry, reflect)


def pack_kernel(
    count, recv_h, src_h, geo_h, emis_h, occ_h, shared, words,
    recv, src, geo, emis, occ, sem,
):
    chunks = emis.shape[1] // LANES
    own = emis.shape[1] // TILE
    me = lax.axis_index("row")
    copies = [
        pltpu.make_async_copy(a, b, sem.at[i])
        for i, (a, b) in enumerate(
            ((recv_h, recv), (src_h, src), (geo_h, geo), (emis_h, emis), (occ_h, occ))
        )
    ]
    for copy in copies:
        copy.start()
    words[...] = jnp.zeros_like(words)
    for copy in copies:
        copy.wait()
    for c in range(chunks):
        lanes = slice(c * LANES, (c + 1) * LANES)
        shared[c * HOURS : (c + 1) * HOURS, :] = emis[:, lanes]
        start = chunks * HOURS + c * SHARED
        shared[start : start + 9, :] = geo[:, lanes]
        shared[start + 9 : start + 10, :] = jnp.zeros((1, LANES), F32)
    lane = lax.broadcasted_iota(jnp.int32, (1, LANES), 1)

    def slot(k, code):
        tile = recv[k]
        owner = tile // own
        row = 2 * (tile - owner * own)
        line = occ[pl.ds(k, 1), :].astype(F32)
        for c in range(2):
            words[owner ^ me, pl.ds(row + c, 1), :] = line[:, c * LANES : (c + 1) * LANES]
        return jnp.where(lane == tile, 1 + src[k], code)

    code = lax.fori_loop(0, count[0], slot, jnp.zeros_like(lane))
    start = chunks * HOURS + 9
    shared[start : start + 1, :] = code.astype(F32)


def pack(geometry, emission, occlusion, pair_recv, pair_src, pair_count):
    vmem = pl.BlockSpec(memory_space=pltpu.VMEM)
    smem = pl.BlockSpec(memory_space=pltpu.SMEM)
    hbm = pl.BlockSpec(memory_space=pltpu.HBM)
    width = geometry.shape[1]
    n_dev = lax.axis_size("row")
    large = [
        pltpu.with_memory_space_constraint(x, pltpu.HBM)
        for x in (pair_recv, pair_src, geometry, emission, occlusion)
    ]
    return pl.pallas_call(
        pack_kernel,
        out_shape=(
            jax.ShapeDtypeStruct((width // LANES * (HOURS + SHARED), LANES), F32),
            jax.ShapeDtypeStruct((n_dev, width // LANES, LANES), F32),
        ),
        in_specs=[smem] + [hbm] * 5,
        out_specs=(vmem, vmem),
        scratch_shapes=[
            pltpu.SMEM(pair_recv.shape, jnp.int32),
            pltpu.SMEM(pair_src.shape, jnp.int32),
            pltpu.VMEM(geometry.shape, F32),
            pltpu.VMEM(emission.shape, F32),
            pltpu.VMEM(occlusion.shape, jnp.int32),
            pltpu.SemaphoreType.DMA((5,)),
        ],
        compiler_params=pltpu.CompilerParams(vmem_limit_bytes=4 << 20),
        name="pack",
    )(pair_count, *large)


def source_factors(geo, origin, exact, rhs1, rhs2, middle):
    centre, offsets, normal, area = frame(geo, origin)
    one = jnp.ones_like(area)
    zero = jnp.zeros_like(area)

    def put(ref, col, rows):
        hi, mid, lo = split3(jnp.concatenate(rows, 0))
        ref[:, col * TILE : (col + 1) * TILE] = jnp.concatenate(
            [hi, mid, lo, hi, mid, hi], 0
        ).astype(BF16)

    if exact:
        m2 = [-2.0 * x for x in centre]
        for q, b in enumerate(offsets):
            rest = dot3(b, b) + 2.0 * dot3(centre, b) + 0.25 * area
            put(rhs1, q, [-2.0 * x for x in b] + m2 + [rest, one])
        put(rhs1, 4, list(normal) + [zero] * 3 + [-dot3(normal, centre), zero])
    else:
        for q, b in enumerate(offsets):
            point = [centre[c] + b[c] for c in range(3)]
            rest = dot3(point, point) + 0.25 * area
            put(rhs1, q, [-2.0 * x for x in point] + [one, rest] + [zero] * 3)
        put(rhs1, 4, list(normal) + [zero, -dot3(normal, centre)] + [zero] * 3)
    weight = area * (1.0 / (16.0 * math.pi))
    for q, b in enumerate(offsets):
        put(
            rhs2,
            q,
            [(centre[c] + b[c]) * weight for c in range(3)] + [weight] + [zero] * 4,
        )
    if exact:
        for c in range(3):
            middle[c : c + 1, :] = centre[c]


def mm(a, b):
    return lax.dot_general(a, b, (((1,), (0,)), ((), ())), preferred_element_type=F32)


def mm_t(a, b):
    return lax.dot_general(a, b, (((1,), (1,)), ((), ())), preferred_element_type=F32)


def inverse_square(t):
    return 1.0 / (t * t)


def block_kernel(
    pay, words, left0, left1, left2, centres, refl, origin_ref,
    blocks, out_b, out_sums, out_scale, order,
    rhs1, rhs2, middle, next1, next2, next_middle, word_s, acc_hi, acc_lo,
    code_v, code, code_sem,
):
    n_dev = pay.shape[0]
    own = refl.shape[1] // TILE
    pairs = own * n_dev
    chunks = refl.shape[1] // LANES
    geo_row = chunks * HOURS
    origin = [origin_ref[c : c + 1, 0:1] for c in range(3)]
    lane = lax.broadcasted_iota(jnp.int32, (1, LANES), 1)
    first = own * lax.axis_index("row")
    wide = lax.broadcasted_iota(jnp.int32, (n_dev, LANES), 1)
    table = jnp.zeros((n_dev, LANES), F32)
    rows = pay[:, geo_row + 9, :]
    for r in range(own):
        here = jnp.sum(jnp.where(lane == first + r, rows, 0.0), 1, keepdims=True)
        table = jnp.where(wide == r, here, table)
    far = [jnp.zeros((n_dev, LANES), F32)] * 3
    for c in range(chunks):
        for part in range(3):
            at = geo_row + SHARED * c + 3 * part
            v = [pay[:, at + x, :] for x in range(3)]
            if part == 0:
                v = [v[x] - origin[x] for x in range(3)]
            far[part] = jnp.maximum(far[part], dot3(v, v))
    reach = sum(jnp.sqrt(jnp.max(f)) for f in far)
    near = 2.0 * reach * reach * 2.0**-23 <= NEAR * 0.25 * AREA_MIN
    code_v[...] = table.astype(jnp.int32)
    to_scalar = pltpu.make_async_copy(code_v, code, code_sem)
    to_scalar.start()
    acc_hi[...] = jnp.zeros_like(acc_hi)
    acc_lo[...] = jnp.zeros_like(acc_lo)
    lane = lax.broadcasted_iota(jnp.int32, (1, TILE), 1)
    group_bit = jnp.left_shift(1, lane // (TILE // GROUPS))
    to_scalar.wait()

    order[0] = 0

    def listed(k, count):
        r = k // n_dev
        value = code[k - r * n_dev, r]
        order[1 + count] = jnp.maximum(value - 1, 0) * pairs + k
        return count + (value > 0).astype(jnp.int32)

    n = lax.fori_loop(0, pairs, listed, jnp.int32(0))
    order[0] = n
    order[1 + n] = 0

    def where_is(i):
        entry = order[1 + i]
        value = entry // pairs
        k = entry - value * pairs
        r = k // n_dev
        return r, k - r * n_dev, value

    def prepare(i, exact):
        _, j, source = where_is(i)
        at = geo_row + 2 * SHARED * source
        geo = [
            jnp.concatenate(
                [pay[j, pl.ds(at + c, 1), :], pay[j, pl.ds(at + SHARED + c, 1), :]], 1
            )
            for c in range(9)
        ]
        source_factors(geo, origin, exact, next1, next2, next_middle)

    def deposit(i):
        r, j, source = where_is(i)
        at = pl.multiple_of(2 * HOURS * source, HOURS)
        x = jnp.concatenate(
            [pay[j, pl.ds(at, HOURS), :], pay[j, pl.ds(at + HOURS, HOURS), :]], 1
        )
        x_hi, x_lo = split2(x)
        ones = jnp.ones((16, TILE), BF16)
        acc_hi[r] += mm_t(jnp.concatenate([x_hi, x_lo, ones], 0), blocks[i, 0])
        acc_lo[r] += mm_t(jnp.concatenate([x_hi, ones], 0), blocks[i, 1])

    def pair(exact, i, carry):
        r, j, _ = where_is(i)
        rhs1[...] = next1[...]
        rhs2[...] = next2[...]
        if exact:
            middle[...] = next_middle[...]
        for c in range(2):
            word_s[c * LANES : (c + 1) * LANES, :] = across(
                words[j, pl.ds(2 * r + c, 1), :].astype(jnp.int32)
            )
        prepare(i + 1, exact)
        for c in range(N_CH):
            rows = slice(c * CH, (c + 1) * CH)
            own_rows = pl.ds(pl.multiple_of(r * TILE + c * CH, CH), CH)
            lhs2 = left2[own_rows, :]
            lhs1 = (left1 if exact else left0)[r * N_CH + c]
            s = None
            for x in range(3 if exact else 0):
                mine = centres[x, own_rows, :]
                d = middle[x : x + 1, :] - jnp.concatenate([mine, mine], 1)
                s = d * d if s is None else s + d * d
            facing = jnp.maximum(mm(lhs1, rhs1[:, 4 * TILE : 5 * TILE]), 0.0)
            total = None
            for q in range(4):
                cols = slice(q * TILE, (q + 1) * TILE)
                rest = mm(lhs1, rhs1[:, cols])
                part = None
                for p in range(4):
                    pr = slice(p * CH, (p + 1) * CH)
                    t = s + rest[pr] if exact else rest[pr]
                    term = facing[pr] * inverse_square(t)
                    part = term if part is None else part + term
                a = jnp.maximum(mm(lhs2, rhs2[:, cols]), 0.0) * part
                total = a if total is None else total + a
            w = word_s[rows, :]
            w = jnp.concatenate([w, w], 1)
            total = jnp.where((w & group_bit) != 0, total, 0.0)
            hi, lo = split2(total)
            blocks[i, 0, rows, :] = hi
            blocks[i, 1, rows, :] = lo
        deposit(i)
        return carry

    for exact in (False, True):

        @pl.when(jnp.logical_not(near) if exact else near)
        def _():
            prepare(0, exact)
            lax.fori_loop(0, n, functools.partial(pair, exact), 0)

    for r in range(own):
        cols = slice(r * TILE, (r + 1) * TILE)
        irr = acc_hi[r, 0:16] + acc_hi[r, 16:32] + acc_lo[r, 0:16]
        sums = acc_hi[r, 32:33] + acc_lo[r, 16:17]
        scale = refl[:, cols] / jnp.maximum(sums, 1.0)
        out_sums[:, cols] = sums
        out_scale[:, cols] = scale
        emis = [pay[0, c * HOURS : (c + 1) * HOURS, :] for c in (2 * r, 2 * r + 1)]
        out_b[:, cols] = jnp.concatenate(emis, 1) + scale * irr


def view_blocks(pay, words, left0, left1, left2, centres, reflect, origin):
    vmem = pl.BlockSpec(memory_space=pltpu.VMEM)
    n_dev = pay.shape[0]
    width = reflect.shape[1]
    own = width // TILE
    pairs = own * n_dev
    return pl.pallas_call(
        block_kernel,
        out_shape=(
            jax.ShapeDtypeStruct((pairs, 2, TILE, TILE), BF16),
            jax.ShapeDtypeStruct((HOURS, width), F32),
            jax.ShapeDtypeStruct((1, width), F32),
            jax.ShapeDtypeStruct((1, width), F32),
            jax.ShapeDtypeStruct((2 * pairs,), jnp.int32),
        ),
        in_specs=[vmem] * 8,
        out_specs=(vmem, vmem, vmem, vmem, pl.BlockSpec(memory_space=pltpu.SMEM)),
        scratch_shapes=[
            pltpu.VMEM((SPLIT_K, 5 * TILE), BF16),
            pltpu.VMEM((SPLIT_K, 4 * TILE), BF16),
            pltpu.VMEM((8, TILE), F32),
            pltpu.VMEM((SPLIT_K, 5 * TILE), BF16),
            pltpu.VMEM((SPLIT_K, 4 * TILE), BF16),
            pltpu.VMEM((8, TILE), F32),
            pltpu.VMEM((TILE, 128), jnp.int32),
            pltpu.VMEM((own, 48, TILE), F32),
            pltpu.VMEM((own, 32, TILE), F32),
            pltpu.VMEM((n_dev, 128), jnp.int32),
            pltpu.SMEM((n_dev, 128), jnp.int32),
            pltpu.SemaphoreType.DMA,
        ],
        compiler_params=pltpu.CompilerParams(vmem_limit_bytes=12 << 20),
        name="view_blocks",
    )(pay, words, left0, left1, left2, centres, reflect, origin)


def bounce_kernel(order, field, blocks, scale, emis, out, acc):
    n_dev = field.shape[0]
    own = out.shape[1] // TILE
    pairs = own * n_dev
    n = order[0]
    acc[...] = jnp.zeros_like(acc)

    def some(step, carry):
        for b in range(4):
            i = 4 * step + b
            live = i < n
            entry = jnp.where(live, order[1 + i], 0)
            value = entry // pairs
            k = entry - value * pairs
            r = k // n_dev
            j = k - r * n_dev
            at = jnp.minimum(i, pairs - 1)
            lanes = pl.ds(pl.multiple_of(value * TILE, TILE), TILE)
            x_hi, x_lo = split2(field[j, :, lanes])
            both = mm_t(jnp.concatenate([x_hi, x_lo], 0), blocks[at, 0])
            got = both[0:16] + both[16:32] + mm_t(x_hi, blocks[at, 1])
            acc[r] += jnp.where(live, got, 0.0)
        return carry

    lax.fori_loop(0, (n + 3) // 4, some, 0)
    for r in range(own):
        cols = slice(r * TILE, (r + 1) * TILE)
        out[:, cols] = emis[:, cols] + scale[:, cols] * acc[r]


def second_bounce(order, field, blocks, scale, emission):
    vmem = pl.BlockSpec(memory_space=pltpu.VMEM)
    own = emission.shape[1] // TILE
    return pl.pallas_call(
        bounce_kernel,
        out_shape=jax.ShapeDtypeStruct(emission.shape, F32),
        in_specs=[pl.BlockSpec(memory_space=pltpu.SMEM)] + [vmem] * 4,
        out_specs=vmem,
        scratch_shapes=[pltpu.VMEM((own, HOURS, TILE), F32)],
        compiler_params=pltpu.CompilerParams(vmem_limit_bytes=12 << 20),
        name="second_bounce",
    )(order, field, blocks, scale, emission)


def gather_rounds(x, n_dev):
    held = x[None]
    step = n_dev // 2
    while step:
        other = lax.ppermute(held, "row", [(i, i ^ step) for i in range(n_dev)])
        held = jnp.concatenate([held, other], 0)
        step //= 2
    return held


def gather_and_deal(shared, words, n_dev, beside):
    held, words = shared[None], words[None]
    step = n_dev // 2
    while step:
        lines = held.shape[0] * held.shape[1]
        keep, send = words[:, :step], words[:, step:]
        message = jnp.concatenate([held.reshape(-1, LANES), send.reshape(-1, LANES)], 0)
        other = lax.ppermute(message, "row", [(i, i ^ step) for i in range(n_dev)])
        if step == 2:
            other, beside = lax.optimization_barrier((other, beside))
        held = jnp.concatenate([held, other[:lines].reshape(held.shape)], 0)
        words = jnp.concatenate([keep, other[lines:].reshape(send.shape)], 0)
        step //= 2
    return held, words[:, 0], beside


def on_device(geometry, emission, reflect, occlusion, pair_recv, pair_src, pair_count):
    n_dev = lax.axis_size("row")
    shared, words = pack(geometry, emission, occlusion, pair_recv, pair_src, pair_count)
    left = recv_factors(geometry, reflect[None])
    pay, words, left = gather_and_deal(shared, words, n_dev, left)
    blocks, field, sums, scale, order = view_blocks(pay, words, *left)
    fields = gather_rounds(field, n_dev)
    radiosity = second_bounce(order, fields, blocks, scale, emission)
    return (radiosity, sums[0])


def solution(mesh):
    placed = (
        P(None, ("grp", "row")),
        P(None, ("grp", "row")),
        P(("grp", "row")),
        P(("grp", "row"), None),
        P(("grp", "row")),
        P(("grp", "row")),
        P(("grp", "row")),
    )
    return jax.shard_map(
        on_device,
        mesh=mesh,
        in_specs=placed,
        out_specs=(P(None, ("grp", "row")), P(("grp", "row"))),
        check_vma=False,
    )
```

```python
import functools
import math

import jax
import jax.numpy as jnp
from jax import lax
from jax.experimental import pallas as pl
from jax.experimental.pallas import tpu as pltpu
from jax.sharding import PartitionSpec as P

TILE = 256
GROUPS = 16
HOURS = 16
CH = 32
N_CH = TILE // CH
SPLIT_K = 48
BF16 = jnp.bfloat16
F32 = jnp.float32

LANES = 128
SHARED = 10
AREA_MIN = 0.2
NEAR = 4e-4


def to_bf16(x):
    return x.astype(BF16).astype(F32)


def split3(x, narrow=to_bf16):
    hi = narrow(x)
    rest = x - hi
    mid = narrow(rest)
    return hi, mid, rest - mid


def split2(x):
    hi = x.astype(BF16)
    return hi, (x - hi.astype(F32)).astype(BF16)


def cross_of(u, v):
    return (
        u[1] * v[2] - u[2] * v[1],
        u[2] * v[0] - u[0] * v[2],
        u[0] * v[1] - u[1] * v[0],
    )


def dot3(a, b):
    return a[0] * b[0] + a[1] * b[1] + a[2] * b[2]


def frame(geo, origin):
    corner = [geo[c] - origin[c] for c in range(3)]
    u = [geo[3 + c] for c in range(3)]
    v = [geo[6 + c] for c in range(3)]
    centre = [corner[c] + 0.5 * (u[c] + v[c]) for c in range(3)]
    e1 = [0.25 * (u[c] + v[c]) for c in range(3)]
    e2 = [0.25 * (u[c] - v[c]) for c in range(3)]
    cross = cross_of(u, v)
    area = jnp.sqrt(dot3(cross, cross))
    normal = [cross[c] / area for c in range(3)]
    offsets = [e1, [-x for x in e1], e2, [-x for x in e2]]
    return centre, offsets, normal, area


def across(row):
    parts = [
        jnp.transpose(jnp.broadcast_to(row[:, c : c + 128], (128, 128)))
        for c in range(0, row.shape[1], 128)
    ]
    return jnp.concatenate(parts, 0)


def recv_kernel(geo_ref, refl, left0, left1, left2, centres, refl_out, middle_out):
    geo = [geo_ref[c : c + 1] for c in range(9)]
    origin = [jnp.mean(geo[c], 1, keepdims=True) for c in range(3)]
    middle_out[...] = jnp.concatenate(
        [jnp.broadcast_to(x, (1, LANES)) for x in origin] + [jnp.zeros((5, LANES), F32)], 0
    )
    centre, offsets, normal, _ = frame(geo, origin)
    one = jnp.ones_like(centre[0])
    zero = jnp.zeros_like(one)

    def columns(rows):
        hi, mid, lo = split3(jnp.concatenate(rows, 0))
        pad = [jnp.zeros_like(hi)] * ((128 - SPLIT_K) // 8)
        wide = jnp.concatenate([hi, hi, hi, mid, mid, lo] + pad, 0)
        return jnp.transpose(wide)[:, :SPLIT_K].astype(BF16)

    for p, a in enumerate(offsets):
        point = [centre[c] + a[c] for c in range(3)]
        cols0 = columns(point + [dot3(point, point), one] + [zero] * 3)
        cols1 = columns(point + list(a) + [one, dot3(a, a) + 2.0 * dot3(centre, a)])
        for c in range(left1.shape[0]):
            rows = slice(c * CH, (c + 1) * CH)
            left0[c, p * CH : (p + 1) * CH, :] = cols0[rows]
            left1[c, p * CH : (p + 1) * CH, :] = cols1[rows]
    left2[...] = columns(list(normal) + [-dot3(normal, centre)] + [zero] * 4)
    for c in range(3):
        centres[c] = across(centre[c])
    refl_out[...] = refl[...]


def recv_factors(geometry, reflect):
    width = geometry.shape[1]
    vmem = pl.BlockSpec(memory_space=pltpu.VMEM)
    return pl.pallas_call(
        recv_kernel,
        out_shape=(
            jax.ShapeDtypeStruct((width // CH, 4 * CH, SPLIT_K), BF16),
            jax.ShapeDtypeStruct((width // CH, 4 * CH, SPLIT_K), BF16),
            jax.ShapeDtypeStruct((width, SPLIT_K), BF16),
            jax.ShapeDtypeStruct((3, width, 128), F32),
            jax.ShapeDtypeStruct((1, width), F32),
            jax.ShapeDtypeStruct((8, LANES), F32),
        ),
        in_specs=[vmem] * 2,
        out_specs=(vmem,) * 6,
        cost_estimate=pl.CostEstimate(flops=200000, bytes_accessed=1600000, transcendentals=1024),
        compiler_params=pltpu.CompilerParams(vmem_limit_bytes=4 << 20),
        name="recv_factors",
    )(geometry, reflect)


def pack_kernel(
    count, recv_h, src_h, geo_h, emis_h, occ_h, shared, words,
    recv, src, geo, emis, occ, sem,
):
    chunks = emis.shape[1] // LANES
    own = emis.shape[1] // TILE
    me = lax.axis_index("row")
    copies = [
        pltpu.make_async_copy(a, b, sem.at[i])
        for i, (a, b) in enumerate(
            ((recv_h, recv), (src_h, src), (geo_h, geo), (emis_h, emis), (occ_h, occ))
        )
    ]
    for copy in copies:
        copy.start()
    words[...] = jnp.zeros_like(words)
    for copy in copies:
        copy.wait()
    for c in range(chunks):
        lanes = slice(c * LANES, (c + 1) * LANES)
        shared[c * HOURS : (c + 1) * HOURS, :] = emis[:, lanes]
        start = chunks * HOURS + c * SHARED
        shared[start : start + 9, :] = geo[:, lanes]
        shared[start + 9 : start + 10, :] = jnp.zeros((1, LANES), F32)
    lane = lax.broadcasted_iota(jnp.int32, (1, LANES), 1)

    def slot(k, code):
        tile = recv[k]
        owner = tile // own
        row = 2 * (tile - owner * own)
        line = occ[pl.ds(k, 1), :].astype(F32)
        for c in range(2):
            words[owner ^ me, pl.ds(row + c, 1), :] = line[:, c * LANES : (c + 1) * LANES]
        return jnp.where(lane == tile, 1 + src[k], code)

    code = lax.fori_loop(0, count[0], slot, jnp.zeros_like(lane))
    start = chunks * HOURS + 9
    shared[start : start + 1, :] = code.astype(F32)


def pack(geometry, emission, occlusion, pair_recv, pair_src, pair_count):
    vmem = pl.BlockSpec(memory_space=pltpu.VMEM)
    smem = pl.BlockSpec(memory_space=pltpu.SMEM)
    hbm = pl.BlockSpec(memory_space=pltpu.HBM)
    width = geometry.shape[1]
    n_dev = lax.axis_size("row")
    large = [
        pltpu.with_memory_space_constraint(x, pltpu.HBM)
        for x in (pair_recv, pair_src, geometry, emission, occlusion)
    ]
    return pl.pallas_call(
        pack_kernel,
        out_shape=(
            jax.ShapeDtypeStruct((width // LANES * (HOURS + SHARED), LANES), F32),
            jax.ShapeDtypeStruct((n_dev, width // LANES, LANES), F32),
        ),
        in_specs=[smem] + [hbm] * 5,
        out_specs=(vmem, vmem),
        scratch_shapes=[
            pltpu.SMEM(pair_recv.shape, jnp.int32),
            pltpu.SMEM(pair_src.shape, jnp.int32),
            pltpu.VMEM(geometry.shape, F32),
            pltpu.VMEM(emission.shape, F32),
            pltpu.VMEM(occlusion.shape, jnp.int32),
            pltpu.SemaphoreType.DMA((5,)),
        ],
        compiler_params=pltpu.CompilerParams(vmem_limit_bytes=4 << 20),
        name="pack",
    )(pair_count, *large)


def source_factors(geo, origin, exact, rhs1, rhs2, middle):
    centre, offsets, normal, area = frame(geo, origin)
    one = jnp.ones_like(area)
    zero = jnp.zeros_like(area)

    def put(ref, col, rows):
        hi, mid, lo = split3(jnp.concatenate(rows, 0))
        ref[:, col * TILE : (col + 1) * TILE] = jnp.concatenate(
            [hi, mid, lo, hi, mid, hi], 0
        ).astype(BF16)

    if exact:
        m2 = [-2.0 * x for x in centre]
        for q, b in enumerate(offsets):
            rest = dot3(b, b) + 2.0 * dot3(centre, b) + 0.25 * area
            put(rhs1, q, [-2.0 * x for x in b] + m2 + [rest, one])
        put(rhs1, 4, list(normal) + [zero] * 3 + [-dot3(normal, centre), zero])
    else:
        for q, b in enumerate(offsets):
            point = [centre[c] + b[c] for c in range(3)]
            rest = dot3(point, point) + 0.25 * area
            put(rhs1, q, [-2.0 * x for x in point] + [one, rest] + [zero] * 3)
        put(rhs1, 4, list(normal) + [zero, -dot3(normal, centre)] + [zero] * 3)
    weight = area * (1.0 / (16.0 * math.pi))
    for q, b in enumerate(offsets):
        put(
            rhs2,
            q,
            [(centre[c] + b[c]) * weight for c in range(3)] + [weight] + [zero] * 4,
        )
    if exact:
        for c in range(3):
            middle[c : c + 1, :] = centre[c]


def mm(a, b):
    return lax.dot_general(a, b, (((1,), (0,)), ((), ())), preferred_element_type=F32)


def mm_t(a, b):
    return lax.dot_general(a, b, (((1,), (1,)), ((), ())), preferred_element_type=F32)


def inverse_square(t):
    return 1.0 / (t * t)


def block_kernel(
    begin, last, pay, words, left0, left1, left2, centres, refl, origin_ref, *refs
):
    if last:
        so_far_hi, so_far_lo, blocks, order, out_b, out_sums, out_scale, *refs = refs
        acc_hi, acc_lo, *refs = refs
    else:
        blocks, order, acc_hi, acc_lo, *refs = refs
    (
        rhs1, rhs2, middle, next1, next2, next_middle, word_s, code_v, code, code_sem,
    ) = refs
    n_dev = pay.shape[0]
    own = refl.shape[1] // TILE
    pairs = own * n_dev
    chunks = refl.shape[1] // LANES
    geo_row = chunks * HOURS
    origin = [origin_ref[c : c + 1, 0:1] for c in range(3)]
    lane = lax.broadcasted_iota(jnp.int32, (1, LANES), 1)
    first = own * lax.axis_index("row")
    wide = lax.broadcasted_iota(jnp.int32, (n_dev, LANES), 1)
    table = jnp.zeros((n_dev, LANES), F32)
    rows = pay[:, geo_row + 9, :]
    for r in range(own):
        here = jnp.sum(jnp.where(lane == first + r, rows, 0.0), 1, keepdims=True)
        table = jnp.where(wide == r, here, table)
    far = [jnp.zeros((n_dev, LANES), F32)] * 3
    for c in range(chunks):
        for part in range(3):
            at = geo_row + SHARED * c + 3 * part
            v = [pay[:, at + x, :] for x in range(3)]
            if part == 0:
                v = [v[x] - origin[x] for x in range(3)]
            far[part] = jnp.maximum(far[part], dot3(v, v))
    reach = sum(jnp.sqrt(jnp.max(f)) for f in far)
    near = 2.0 * reach * reach * 2.0**-23 <= NEAR * 0.25 * AREA_MIN
    code_v[...] = table.astype(jnp.int32)
    to_scalar = pltpu.make_async_copy(code_v, code, code_sem)
    to_scalar.start()
    acc_hi[...] = so_far_hi[...] if last else jnp.zeros_like(acc_hi)
    acc_lo[...] = so_far_lo[...] if last else jnp.zeros_like(acc_lo)
    lane = lax.broadcasted_iota(jnp.int32, (1, TILE), 1)
    group_bit = jnp.left_shift(1, lane // (TILE // GROUPS))
    to_scalar.wait()

    order[0] = 0

    n = jnp.int32(0)
    for r in range(own):

        def listed(j, count):
            value = code[j, r]
            order[1 + count] = jnp.maximum(value - 1, 0) * pairs + r * n_dev + j
            return count + (value > 0).astype(jnp.int32)

        n = lax.fori_loop(begin, n_dev, listed, n, unroll=4)
    order[0] = n
    order[1 + n] = 0

    def where_is(i):
        entry = order[1 + i]
        value = entry // pairs
        k = entry - value * pairs
        r = k // n_dev
        return r, k - r * n_dev, value

    def prepare(i, exact):
        _, j, source = where_is(i)
        at = geo_row + 2 * SHARED * source
        geo = [
            jnp.concatenate(
                [pay[j, pl.ds(at + c, 1), :], pay[j, pl.ds(at + SHARED + c, 1), :]], 1
            )
            for c in range(9)
        ]
        source_factors(geo, origin, exact, next1, next2, next_middle)

    def deposit(i):
        r, j, source = where_is(i)
        at = pl.multiple_of(2 * HOURS * source, HOURS)
        x = jnp.concatenate(
            [pay[j, pl.ds(at, HOURS), :], pay[j, pl.ds(at + HOURS, HOURS), :]], 1
        )
        x_hi, x_lo = split2(x)
        ones = jnp.ones((16, TILE), BF16)
        acc_hi[r] += mm_t(jnp.concatenate([x_hi, x_lo, ones], 0), blocks[i, 0])
        acc_lo[r] += mm_t(jnp.concatenate([x_hi, ones], 0), blocks[i, 1])

    def pair(exact, i, carry):
        r, j, _ = where_is(i)
        rhs1[...] = next1[...]
        rhs2[...] = next2[...]
        if exact:
            middle[...] = next_middle[...]
        for c in range(2):
            word_s[c * LANES : (c + 1) * LANES, :] = across(
                words[j, pl.ds(2 * r + c, 1), :].astype(jnp.int32)
            )
        prepare(i + 1, exact)
        for c in range(N_CH):
            rows = slice(c * CH, (c + 1) * CH)
            own_rows = pl.ds(pl.multiple_of(r * TILE + c * CH, CH), CH)
            lhs2 = left2[own_rows, :]
            lhs1 = (left1 if exact else left0)[r * N_CH + c]
            s = None
            for x in range(3 if exact else 0):
                mine = centres[x, own_rows, :]
                d = middle[x : x + 1, :] - jnp.concatenate([mine, mine], 1)
                s = d * d if s is None else s + d * d
            facing = jnp.maximum(mm(lhs1, rhs1[:, 4 * TILE : 5 * TILE]), 0.0)
            total = None
            for q in range(4):
                cols = slice(q * TILE, (q + 1) * TILE)
                rest = mm(lhs1, rhs1[:, cols])
                part = None
                for p in range(4):
                    pr = slice(p * CH, (p + 1) * CH)
                    t = s + rest[pr] if exact else rest[pr]
                    term = facing[pr] * inverse_square(t)
                    part = term if part is None else part + term
                a = jnp.maximum(mm(lhs2, rhs2[:, cols]), 0.0) * part
                total = a if total is None else total + a
            w = word_s[rows, :]
            w = jnp.concatenate([w, w], 1)
            total = jnp.where((w & group_bit) != 0, total, 0.0)
            hi, lo = split2(total)
            blocks[i, 0, rows, :] = hi
            blocks[i, 1, rows, :] = lo
        deposit(i)
        return carry

    for exact in (False, True):

        @pl.when(jnp.logical_not(near) if exact else near)
        def _():
            prepare(0, exact)
            lax.fori_loop(0, n, functools.partial(pair, exact), 0)

    if not last:
        return
    for r in range(own):
        cols = slice(r * TILE, (r + 1) * TILE)
        irr = acc_hi[r, 0:16] + acc_hi[r, 16:32] + acc_lo[r, 0:16]
        sums = acc_hi[r, 32:33] + acc_lo[r, 16:17]
        scale = refl[:, cols] / jnp.maximum(sums, 1.0)
        out_sums[:, cols] = sums
        out_scale[:, cols] = scale
        emis = [pay[0, c * HOURS : (c + 1) * HOURS, :] for c in (2 * r, 2 * r + 1)]
        out_b[:, cols] = jnp.concatenate(emis, 1) + scale * irr


def view_blocks(begin, pay, words, left, so_far=None):
    vmem = pl.BlockSpec(memory_space=pltpu.VMEM)
    n_dev = pay.shape[0]
    width = left[4].shape[1]
    own = width // TILE
    pairs = own * n_dev
    sums = [
        jax.ShapeDtypeStruct((own, 48, TILE), F32),
        jax.ShapeDtypeStruct((own, 32, TILE), F32),
    ]
    outs = [
        jax.ShapeDtypeStruct((own * (n_dev - begin), 2, TILE, TILE), BF16),
        jax.ShapeDtypeStruct((2 * pairs,), jnp.int32),
    ]
    scratch = []
    if so_far is None:
        outs += sums
    else:
        outs += [jax.ShapeDtypeStruct((x, width), F32) for x in (HOURS, 1, 1)]
        scratch += [pltpu.VMEM(x.shape, F32) for x in sums]
    args = [pay, words, *left, *(so_far or ())]
    work = own * (n_dev - begin) // 2
    return pl.pallas_call(
        functools.partial(block_kernel, begin, so_far is not None),
        out_shape=outs,
        in_specs=[vmem] * len(args),
        out_specs=[vmem, pl.BlockSpec(memory_space=pltpu.SMEM)] + [vmem] * (len(outs) - 2),
        scratch_shapes=scratch
        + [
            pltpu.VMEM((SPLIT_K, 5 * TILE), BF16),
            pltpu.VMEM((SPLIT_K, 4 * TILE), BF16),
            pltpu.VMEM((8, TILE), F32),
            pltpu.VMEM((SPLIT_K, 5 * TILE), BF16),
            pltpu.VMEM((SPLIT_K, 4 * TILE), BF16),
            pltpu.VMEM((8, TILE), F32),
            pltpu.VMEM((TILE, 128), jnp.int32),
            pltpu.VMEM((n_dev, 128), jnp.int32),
            pltpu.SMEM((n_dev, 128), jnp.int32),
            pltpu.SemaphoreType.DMA,
        ],
        compiler_params=pltpu.CompilerParams(vmem_limit_bytes=12 << 20),
        cost_estimate=pl.CostEstimate(
            flops=work * 10**9, bytes_accessed=work << 18, transcendentals=work << 20
        ),
        name="view_blocks",
    )(*args)


def bounce_kernel(order0, order1, field, blocks0, blocks1, scale, emis, out, acc):
    own = out.shape[1] // TILE
    acc[...] = jnp.zeros_like(acc)

    def some(order, blocks, step, carry):
        pairs = order.shape[0] // 2
        n_dev = pairs // own
        for b in range(4):
            i = 4 * step + b
            live = i < order[0]
            entry = jnp.where(live, order[jnp.minimum(1 + i, 2 * pairs - 1)], 0)
            source = entry // pairs
            k = entry - source * pairs
            r = k // n_dev
            j = k - r * n_dev
            at = jnp.minimum(i, blocks.shape[0] - 1)
            lanes = pl.ds(pl.multiple_of(source * TILE, TILE), TILE)
            x_hi, x_lo = split2(field[j, :, lanes])
            both = mm_t(jnp.concatenate([x_hi, x_lo], 0), blocks[at, 0])
            got = both[0:16] + both[16:32] + mm_t(x_hi, blocks[at, 1])
            acc[r] += jnp.where(live, got, 0.0)
        return carry

    for order, blocks in ((order0, blocks0), (order1, blocks1)):
        lax.fori_loop(0, (order[0] + 3) // 4, functools.partial(some, order, blocks), 0)
    for r in range(own):
        cols = slice(r * TILE, (r + 1) * TILE)
        out[:, cols] = emis[:, cols] + scale[:, cols] * acc[r]


def second_bounce(orders, field, blocks, scale, emission):
    vmem = pl.BlockSpec(memory_space=pltpu.VMEM)
    own = emission.shape[1] // TILE
    return pl.pallas_call(
        bounce_kernel,
        out_shape=jax.ShapeDtypeStruct(emission.shape, F32),
        in_specs=[pl.BlockSpec(memory_space=pltpu.SMEM)] * 2 + [vmem] * 5,
        out_specs=vmem,
        scratch_shapes=[pltpu.VMEM((own, HOURS, TILE), F32)],
        compiler_params=pltpu.CompilerParams(vmem_limit_bytes=12 << 20),
        name="second_bounce",
    )(*orders, field, *blocks, scale, emission)


def gather_rounds(x, n_dev):
    held = x[None]
    step = n_dev // 2
    while step:
        other = lax.ppermute(held, "row", [(i, i ^ step) for i in range(n_dev)])
        held = jnp.concatenate([held, other], 0)
        step //= 2
    return held


def on_device(geometry, emission, reflect, occlusion, pair_recv, pair_src, pair_count):
    n_dev = lax.axis_size("row")
    shared, words = pack(geometry, emission, occlusion, pair_recv, pair_src, pair_count)
    left = recv_factors(geometry, reflect[None])
    held, words = shared[None], words[None]
    step = n_dev // 2
    while step:
        lines = held.shape[0] * held.shape[1]
        keep, send = words[:, :step], words[:, step:]
        message = jnp.concatenate([held.reshape(-1, LANES), send.reshape(-1, LANES)], 0)
        other = lax.ppermute(message, "row", [(i, i ^ step) for i in range(n_dev)])
        if step == n_dev // 4:
            other, left = lax.optimization_barrier((other, left))
        if step == 2:
            begin = held.shape[0]
            early = view_blocks(0, held, words[:, 0], left)
            other, early = lax.optimization_barrier((other, early))
        held = jnp.concatenate([held, other[:lines].reshape(held.shape)], 0)
        words = jnp.concatenate([keep, other[lines:].reshape(send.shape)], 0)
        step //= 2
    blocks0, order0, *so_far = early
    blocks1, order1, field, sums, scale = view_blocks(
        begin, held, words[:, 0], left, so_far
    )
    fields = gather_rounds(field, n_dev)
    radiosity = second_bounce(
        (order0, order1), fields, (blocks0, blocks1), scale, emission
    )
    return (radiosity, sums[0])


def solution(mesh):
    placed = (
        P(None, ("grp", "row")),
        P(None, ("grp", "row")),
        P(("grp", "row")),
        P(("grp", "row"), None),
        P(("grp", "row")),
        P(("grp", "row")),
        P(("grp", "row")),
    )
    return jax.shard_map(
        on_device,
        mesh=mesh,
        in_specs=placed,
        out_specs=(P(None, ("grp", "row")), P(("grp", "row"))),
        check_vma=False,
    )
```

```python
import functools
import math

import jax
import jax.numpy as jnp
from jax import lax
from jax.experimental import pallas as pl
from jax.experimental.pallas import tpu as pltpu
from jax.sharding import PartitionSpec as P

TILE = 256
GROUPS = 16
HOURS = 16
CH = 32
N_CH = TILE // CH
SPLIT_K = 48
BF16 = jnp.bfloat16
F32 = jnp.float32

LANES = 128
SHARED = 10
AREA_MIN = 0.2
NEAR = 4e-4


def to_bf16(x):
    return x.astype(BF16).astype(F32)


def split3(x, narrow=to_bf16):
    hi = narrow(x)
    rest = x - hi
    mid = narrow(rest)
    return hi, mid, rest - mid


def split2(x):
    hi = x.astype(BF16)
    return hi, (x - hi.astype(F32)).astype(BF16)


def cross_of(u, v):
    return (
        u[1] * v[2] - u[2] * v[1],
        u[2] * v[0] - u[0] * v[2],
        u[0] * v[1] - u[1] * v[0],
    )


def dot3(a, b):
    return a[0] * b[0] + a[1] * b[1] + a[2] * b[2]


def frame(geo, origin):
    corner = [geo[c] - origin[c] for c in range(3)]
    u = [geo[3 + c] for c in range(3)]
    v = [geo[6 + c] for c in range(3)]
    centre = [corner[c] + 0.5 * (u[c] + v[c]) for c in range(3)]
    e1 = [0.25 * (u[c] + v[c]) for c in range(3)]
    e2 = [0.25 * (u[c] - v[c]) for c in range(3)]
    cross = cross_of(u, v)
    area = jnp.sqrt(dot3(cross, cross))
    normal = [cross[c] / area for c in range(3)]
    offsets = [e1, [-x for x in e1], e2, [-x for x in e2]]
    return centre, offsets, normal, area


def across(row):
    parts = [
        jnp.transpose(jnp.broadcast_to(row[:, c : c + 128], (128, 128)))
        for c in range(0, row.shape[1], 128)
    ]
    return jnp.concatenate(parts, 0)


def recv_kernel(geo_ref, refl, left0, left1, left2, centres, refl_out, middle_out):
    geo = [geo_ref[c : c + 1] for c in range(9)]
    origin = [jnp.mean(geo[c], 1, keepdims=True) for c in range(3)]
    middle_out[...] = jnp.concatenate(
        [jnp.broadcast_to(x, (1, LANES)) for x in origin] + [jnp.zeros((5, LANES), F32)], 0
    )
    centre, offsets, normal, _ = frame(geo, origin)
    one = jnp.ones_like(centre[0])
    zero = jnp.zeros_like(one)

    def columns(rows):
        hi, mid, lo = split3(jnp.concatenate(rows, 0))
        pad = [jnp.zeros_like(hi)] * ((128 - SPLIT_K) // 8)
        wide = jnp.concatenate([hi, hi, hi, mid, mid, lo] + pad, 0)
        return jnp.transpose(wide)[:, :SPLIT_K].astype(BF16)

    for p, a in enumerate(offsets):
        point = [centre[c] + a[c] for c in range(3)]
        cols0 = columns(point + [dot3(point, point), one] + [zero] * 3)
        cols1 = columns(point + list(a) + [one, dot3(a, a) + 2.0 * dot3(centre, a)])
        for c in range(left1.shape[0]):
            rows = slice(c * CH, (c + 1) * CH)
            left0[c, p * CH : (p + 1) * CH, :] = cols0[rows]
            left1[c, p * CH : (p + 1) * CH, :] = cols1[rows]
    left2[...] = columns(list(normal) + [-dot3(normal, centre)] + [zero] * 4)
    for c in range(3):
        centres[c] = across(centre[c])
    refl_out[...] = refl[...]


def recv_factors(geometry, reflect):
    width = geometry.shape[1]
    vmem = pl.BlockSpec(memory_space=pltpu.VMEM)
    return pl.pallas_call(
        recv_kernel,
        out_shape=(
            jax.ShapeDtypeStruct((width // CH, 4 * CH, SPLIT_K), BF16),
            jax.ShapeDtypeStruct((width // CH, 4 * CH, SPLIT_K), BF16),
            jax.ShapeDtypeStruct((width, SPLIT_K), BF16),
            jax.ShapeDtypeStruct((3, width, 128), F32),
            jax.ShapeDtypeStruct((1, width), F32),
            jax.ShapeDtypeStruct((8, LANES), F32),
        ),
        in_specs=[vmem] * 2,
        out_specs=(vmem,) * 6,
        cost_estimate=pl.CostEstimate(flops=200000, bytes_accessed=1600000, transcendentals=1024),
        compiler_params=pltpu.CompilerParams(vmem_limit_bytes=4 << 20),
        name="recv_factors",
    )(geometry, reflect)


def pack_kernel(
    count, recv_h, src_h, geo_h, emis_h, occ_h, shared, words,
    recv, src, geo, emis, occ, sem,
):
    chunks = emis.shape[1] // LANES
    own = emis.shape[1] // TILE
    me = lax.axis_index("row")
    copies = [
        pltpu.make_async_copy(a, b, sem.at[i])
        for i, (a, b) in enumerate(
            ((recv_h, recv), (src_h, src), (geo_h, geo), (emis_h, emis), (occ_h, occ))
        )
    ]
    for copy in copies:
        copy.start()
    words[...] = jnp.zeros_like(words)
    for copy in copies:
        copy.wait()
    for c in range(chunks):
        lanes = slice(c * LANES, (c + 1) * LANES)
        shared[c * HOURS : (c + 1) * HOURS, :] = emis[:, lanes]
        start = chunks * HOURS + c * SHARED
        shared[start : start + 9, :] = geo[:, lanes]
        shared[start + 9 : start + 10, :] = jnp.zeros((1, LANES), F32)
    lane = lax.broadcasted_iota(jnp.int32, (1, LANES), 1)

    def slot(k, code):
        tile = recv[k]
        owner = tile // own
        row = 2 * (tile - owner * own)
        line = occ[pl.ds(k, 1), :].astype(F32)
        for c in range(2):
            words[owner ^ me, pl.ds(row + c, 1), :] = line[:, c * LANES : (c + 1) * LANES]
        return jnp.where(lane == tile, 1 + src[k], code)

    code = lax.fori_loop(0, count[0], slot, jnp.zeros_like(lane))
    start = chunks * HOURS + 9
    shared[start : start + 1, :] = code.astype(F32)


def pack(geometry, emission, occlusion, pair_recv, pair_src, pair_count):
    vmem = pl.BlockSpec(memory_space=pltpu.VMEM)
    smem = pl.BlockSpec(memory_space=pltpu.SMEM)
    hbm = pl.BlockSpec(memory_space=pltpu.HBM)
    width = geometry.shape[1]
    n_dev = lax.axis_size("row")
    large = [
        pltpu.with_memory_space_constraint(x, pltpu.HBM)
        for x in (pair_recv, pair_src, geometry, emission, occlusion)
    ]
    return pl.pallas_call(
        pack_kernel,
        out_shape=(
            jax.ShapeDtypeStruct((width // LANES * (HOURS + SHARED), LANES), F32),
            jax.ShapeDtypeStruct((n_dev, width // LANES, LANES), F32),
        ),
        in_specs=[smem] + [hbm] * 5,
        out_specs=(vmem, vmem),
        scratch_shapes=[
            pltpu.SMEM(pair_recv.shape, jnp.int32),
            pltpu.SMEM(pair_src.shape, jnp.int32),
            pltpu.VMEM(geometry.shape, F32),
            pltpu.VMEM(emission.shape, F32),
            pltpu.VMEM(occlusion.shape, jnp.int32),
            pltpu.SemaphoreType.DMA((5,)),
        ],
        compiler_params=pltpu.CompilerParams(vmem_limit_bytes=4 << 20),
        name="pack",
    )(pair_count, *large)


def source_factors(geo, origin, exact, rhs1, rhs2, middle):
    centre, offsets, normal, area = frame(geo, origin)
    one = jnp.ones_like(area)
    zero = jnp.zeros_like(area)

    def put(ref, col, rows):
        hi, mid, lo = split3(jnp.concatenate(rows, 0))
        ref[:, col * TILE : (col + 1) * TILE] = jnp.concatenate(
            [hi, mid, lo, hi, mid, hi], 0
        ).astype(BF16)

    if exact:
        m2 = [-2.0 * x for x in centre]
        for q, b in enumerate(offsets):
            rest = dot3(b, b) + 2.0 * dot3(centre, b) + 0.25 * area
            put(rhs1, q, [-2.0 * x for x in b] + m2 + [rest, one])
        put(rhs1, 4, list(normal) + [zero] * 3 + [-dot3(normal, centre), zero])
    else:
        for q, b in enumerate(offsets):
            point = [centre[c] + b[c] for c in range(3)]
            rest = dot3(point, point) + 0.25 * area
            put(rhs1, q, [-2.0 * x for x in point] + [one, rest] + [zero] * 3)
        put(rhs1, 4, list(normal) + [zero, -dot3(normal, centre)] + [zero] * 3)
    weight = area * (1.0 / (16.0 * math.pi))
    for q, b in enumerate(offsets):
        put(
            rhs2,
            q,
            [(centre[c] + b[c]) * weight for c in range(3)] + [weight] + [zero] * 4,
        )
    if exact:
        for c in range(3):
            middle[c : c + 1, :] = centre[c]


def mm(a, b):
    return lax.dot_general(a, b, (((1,), (0,)), ((), ())), preferred_element_type=F32)


def mm_t(a, b):
    return lax.dot_general(a, b, (((1,), (1,)), ((), ())), preferred_element_type=F32)


def inverse_square(t):
    return 1.0 / (t * t)


def block_kernel(
    begin, last, pay, words, left0, left1, left2, centres, refl, origin_ref, *refs
):
    if begin:
        so_far_hi, so_far_lo, *refs = refs
    blocks, order, *refs = refs
    if last:
        out_b, out_sums, out_scale, *refs = refs
    acc_hi, acc_lo, *refs = refs
    (
        rhs1, rhs2, middle, next1, next2, next_middle, word_s, code_v, code, code_sem,
    ) = refs
    n_dev = pay.shape[0]
    own = refl.shape[1] // TILE
    pairs = own * n_dev
    chunks = refl.shape[1] // LANES
    geo_row = chunks * HOURS
    origin = [origin_ref[c : c + 1, 0:1] for c in range(3)]
    lane = lax.broadcasted_iota(jnp.int32, (1, LANES), 1)
    first = own * lax.axis_index("row")
    wide = lax.broadcasted_iota(jnp.int32, (n_dev, LANES), 1)
    table = jnp.zeros((n_dev, LANES), F32)
    rows = pay[:, geo_row + 9, :]
    for r in range(own):
        here = jnp.sum(jnp.where(lane == first + r, rows, 0.0), 1, keepdims=True)
        table = jnp.where(wide == r, here, table)
    far = [jnp.zeros((n_dev, LANES), F32)] * 3
    for c in range(chunks):
        for part in range(3):
            at = geo_row + SHARED * c + 3 * part
            v = [pay[:, at + x, :] for x in range(3)]
            if part == 0:
                v = [v[x] - origin[x] for x in range(3)]
            far[part] = jnp.maximum(far[part], dot3(v, v))
    reach = sum(jnp.sqrt(jnp.max(f)) for f in far)
    near = 2.0 * reach * reach * 2.0**-23 <= NEAR * 0.25 * AREA_MIN
    code_v[...] = table.astype(jnp.int32)
    to_scalar = pltpu.make_async_copy(code_v, code, code_sem)
    to_scalar.start()
    acc_hi[...] = so_far_hi[...] if begin else jnp.zeros_like(acc_hi)
    acc_lo[...] = so_far_lo[...] if begin else jnp.zeros_like(acc_lo)
    lane = lax.broadcasted_iota(jnp.int32, (1, TILE), 1)
    group_bit = jnp.left_shift(1, lane // (TILE // GROUPS))
    to_scalar.wait()

    order[0] = 0

    n = jnp.int32(0)
    for r in range(own):

        def listed(j, count):
            value = code[j, r]
            order[1 + count] = jnp.maximum(value - 1, 0) * pairs + r * n_dev + j
            return count + (value > 0).astype(jnp.int32)

        n = lax.fori_loop(begin, n_dev, listed, n, unroll=4)
    order[0] = n
    order[1 + n] = 0

    def where_is(i):
        entry = order[1 + i]
        value = entry // pairs
        k = entry - value * pairs
        r = k // n_dev
        return r, k - r * n_dev, value

    def prepare(i, exact):
        _, j, source = where_is(i)
        at = geo_row + 2 * SHARED * source
        geo = [
            jnp.concatenate(
                [pay[j, pl.ds(at + c, 1), :], pay[j, pl.ds(at + SHARED + c, 1), :]], 1
            )
            for c in range(9)
        ]
        source_factors(geo, origin, exact, next1, next2, next_middle)

    def deposit(i, real):
        i = jnp.maximum(i, 0)
        r, j, source = where_is(i)
        at = pl.multiple_of(2 * HOURS * source, HOURS)
        x = jnp.concatenate(
            [pay[j, pl.ds(at, HOURS), :], pay[j, pl.ds(at + HOURS, HOURS), :]], 1
        )
        x_hi, x_lo = split2(x)
        ones = jnp.ones((16, TILE), BF16)
        hi = mm_t(jnp.concatenate([x_hi, x_lo, ones], 0), blocks[i, 0])
        lo = mm_t(jnp.concatenate([x_hi, ones], 0), blocks[i, 1])
        acc_hi[r] += jnp.where(real, hi, 0.0)
        acc_lo[r] += jnp.where(real, lo, 0.0)

    def pair(exact, i, carry):
        r, j, _ = where_is(i)
        rhs1[...] = next1[...]
        rhs2[...] = next2[...]
        if exact:
            middle[...] = next_middle[...]
        for c in range(2):
            word_s[c * LANES : (c + 1) * LANES, :] = across(
                words[j, pl.ds(2 * r + c, 1), :].astype(jnp.int32)
            )
        deposit(i - 1, i > 0)
        prepare(i + 1, exact)
        for c in range(N_CH):
            rows = slice(c * CH, (c + 1) * CH)
            own_rows = pl.ds(pl.multiple_of(r * TILE + c * CH, CH), CH)
            lhs2 = left2[own_rows, :]
            lhs1 = (left1 if exact else left0)[r * N_CH + c]
            s = None
            for x in range(3 if exact else 0):
                mine = centres[x, own_rows, :]
                d = middle[x : x + 1, :] - jnp.concatenate([mine, mine], 1)
                s = d * d if s is None else s + d * d
            facing = jnp.maximum(mm(lhs1, rhs1[:, 4 * TILE : 5 * TILE]), 0.0)
            total = None
            for q in range(4):
                cols = slice(q * TILE, (q + 1) * TILE)
                rest = mm(lhs1, rhs1[:, cols])
                part = None
                for p in range(4):
                    pr = slice(p * CH, (p + 1) * CH)
                    t = s + rest[pr] if exact else rest[pr]
                    term = facing[pr] * inverse_square(t)
                    part = term if part is None else part + term
                a = jnp.maximum(mm(lhs2, rhs2[:, cols]), 0.0) * part
                total = a if total is None else total + a
            w = word_s[rows, :]
            w = jnp.concatenate([w, w], 1)
            total = jnp.where((w & group_bit) != 0, total, 0.0)
            hi, lo = split2(total)
            blocks[i, 0, rows, :] = hi
            blocks[i, 1, rows, :] = lo
        return carry

    for exact in (False, True):

        @pl.when(jnp.logical_not(near) if exact else near)
        def _():
            prepare(0, exact)
            lax.fori_loop(0, n, functools.partial(pair, exact), 0)

    deposit(n - 1, n > 0)
    if not last:
        return
    for r in range(own):
        cols = slice(r * TILE, (r + 1) * TILE)
        irr = acc_hi[r, 0:16] + acc_hi[r, 16:32] + acc_lo[r, 0:16]
        sums = acc_hi[r, 32:33] + acc_lo[r, 16:17]
        scale = refl[:, cols] / jnp.maximum(sums, 1.0)
        out_sums[:, cols] = sums
        out_scale[:, cols] = scale
        emis = [pay[0, c * HOURS : (c + 1) * HOURS, :] for c in (2 * r, 2 * r + 1)]
        out_b[:, cols] = jnp.concatenate(emis, 1) + scale * irr


def view_blocks(begin, last, pay, words, left, so_far):
    vmem = pl.BlockSpec(memory_space=pltpu.VMEM)
    n_dev = pay.shape[0]
    width = left[4].shape[1]
    own = width // TILE
    pairs = own * n_dev
    sums = [
        jax.ShapeDtypeStruct((own, 48, TILE), F32),
        jax.ShapeDtypeStruct((own, 32, TILE), F32),
    ]
    outs = [
        jax.ShapeDtypeStruct((own * (n_dev - begin), 2, TILE, TILE), BF16),
        jax.ShapeDtypeStruct((2 * pairs,), jnp.int32),
    ]
    scratch = []
    if not last:
        outs += sums
    else:
        outs += [jax.ShapeDtypeStruct((x, width), F32) for x in (HOURS, 1, 1)]
        scratch += [pltpu.VMEM(x.shape, F32) for x in sums]
    args = [pay, words, *left, *so_far]
    work = own * (n_dev - begin) // 2
    return pl.pallas_call(
        functools.partial(block_kernel, begin, last),
        out_shape=outs,
        in_specs=[vmem] * len(args),
        out_specs=[vmem, pl.BlockSpec(memory_space=pltpu.SMEM)] + [vmem] * (len(outs) - 2),
        scratch_shapes=scratch
        + [
            pltpu.VMEM((SPLIT_K, 5 * TILE), BF16),
            pltpu.VMEM((SPLIT_K, 4 * TILE), BF16),
            pltpu.VMEM((8, TILE), F32),
            pltpu.VMEM((SPLIT_K, 5 * TILE), BF16),
            pltpu.VMEM((SPLIT_K, 4 * TILE), BF16),
            pltpu.VMEM((8, TILE), F32),
            pltpu.VMEM((TILE, 128), jnp.int32),
            pltpu.VMEM((n_dev, 128), jnp.int32),
            pltpu.SMEM((n_dev, 128), jnp.int32),
            pltpu.SemaphoreType.DMA,
        ],
        compiler_params=pltpu.CompilerParams(vmem_limit_bytes=12 << 20),
        cost_estimate=pl.CostEstimate(
            flops=work * 10**9, bytes_accessed=work << 18, transcendentals=work << 20
        ),
        name="view_blocks",
    )(*args)


def bounce_kernel(field, scale, emis, *refs):
    *lists, out, acc = refs
    own = out.shape[1] // TILE
    acc[...] = jnp.zeros_like(acc)

    def some(order, blocks, step, carry):
        pairs = order.shape[0] // 2
        n_dev = pairs // own
        for b in range(4):
            i = 4 * step + b
            live = i < order[0]
            entry = jnp.where(live, order[jnp.minimum(1 + i, 2 * pairs - 1)], 0)
            source = entry // pairs
            k = entry - source * pairs
            r = k // n_dev
            j = k - r * n_dev
            at = jnp.minimum(i, blocks.shape[0] - 1)
            lanes = pl.ds(pl.multiple_of(source * TILE, TILE), TILE)
            x_hi, x_lo = split2(field[j, :, lanes])
            both = mm_t(jnp.concatenate([x_hi, x_lo], 0), blocks[at, 0])
            got = both[0:16] + both[16:32] + mm_t(x_hi, blocks[at, 1])
            acc[r] += jnp.where(live, got, 0.0)
        return carry

    for blocks, order in zip(lists[0::2], lists[1::2]):
        lax.fori_loop(0, (order[0] + 3) // 4, functools.partial(some, order, blocks), 0)
    for r in range(own):
        cols = slice(r * TILE, (r + 1) * TILE)
        out[:, cols] = emis[:, cols] + scale[:, cols] * acc[r]


def second_bounce(done, field, scale, emission):
    vmem = pl.BlockSpec(memory_space=pltpu.VMEM)
    own = emission.shape[1] // TILE
    return pl.pallas_call(
        bounce_kernel,
        out_shape=jax.ShapeDtypeStruct(emission.shape, F32),
        in_specs=[vmem] * 3 + [vmem, pl.BlockSpec(memory_space=pltpu.SMEM)] * len(done),
        out_specs=vmem,
        scratch_shapes=[pltpu.VMEM((own, HOURS, TILE), F32)],
        compiler_params=pltpu.CompilerParams(vmem_limit_bytes=12 << 20),
        name="second_bounce",
    )(field, scale, emission, *sum(done, ()))


def gather_rounds(x, n_dev):
    held = x[None]
    step = n_dev // 2
    while step:
        other = lax.ppermute(held, "row", [(i, i ^ step) for i in range(n_dev)])
        held = jnp.concatenate([held, other], 0)
        step //= 2
    return held


def on_device(geometry, emission, reflect, occlusion, pair_recv, pair_src, pair_count):
    n_dev = lax.axis_size("row")
    shared, words = pack(geometry, emission, occlusion, pair_recv, pair_src, pair_count)
    left = recv_factors(geometry, reflect[None])
    held, words = shared[None], words[None]
    done, so_far, begin = [], [], 0
    step = n_dev // 2
    while step:
        lines = held.shape[0] * held.shape[1]
        keep, send = words[:, :step], words[:, step:]
        message = jnp.concatenate([held.reshape(-1, LANES), send.reshape(-1, LANES)], 0)
        other = lax.ppermute(message, "row", [(i, i ^ step) for i in range(n_dev)])
        if step == n_dev // 2:
            other, left = lax.optimization_barrier((other, left))
        elif step == 2:
            early = view_blocks(begin, False, held, words[:, 0], left, so_far)
            other, early = lax.optimization_barrier((other, early))
            done.append(tuple(early[:2]))
            so_far = early[2:]
            begin = held.shape[0]
        held = jnp.concatenate([held, other[:lines].reshape(held.shape)], 0)
        words = jnp.concatenate([keep, other[lines:].reshape(send.shape)], 0)
        step //= 2
    blocks, order, field, sums, scale = view_blocks(
        begin, True, held, words[:, 0], left, so_far
    )
    done.append((blocks, order))
    fields = gather_rounds(field, n_dev)
    radiosity = second_bounce(done, fields, scale, emission)
    return (radiosity, sums[0])


def solution(mesh):
    placed = (
        P(None, ("grp", "row")),
        P(None, ("grp", "row")),
        P(("grp", "row")),
        P(("grp", "row"), None),
        P(("grp", "row")),
        P(("grp", "row")),
        P(("grp", "row")),
    )
    return jax.shard_map(
        on_device,
        mesh=mesh,
        in_specs=placed,
        out_specs=(P(None, ("grp", "row")), P(("grp", "row"))),
        check_vma=False,
    )
```

```python
import functools
import math

import jax
import jax.numpy as jnp
from jax import lax
from jax.experimental import pallas as pl
from jax.experimental.pallas import tpu as pltpu
from jax.sharding import PartitionSpec as P

TILE = 256
GROUPS = 16
HOURS = 16
CH = 32
N_CH = TILE // CH
SPLIT_K = 48
BF16 = jnp.bfloat16
F32 = jnp.float32

LANES = 128
SHARED = 10
AREA_MIN = 0.2
NEAR = 4e-4


def to_bf16(x):
    return x.astype(BF16).astype(F32)


def split3(x, narrow=to_bf16):
    hi = narrow(x)
    rest = x - hi
    mid = narrow(rest)
    return hi, mid, rest - mid


def split2(x):
    hi = x.astype(BF16)
    return hi, (x - hi.astype(F32)).astype(BF16)


def cross_of(u, v):
    return (
        u[1] * v[2] - u[2] * v[1],
        u[2] * v[0] - u[0] * v[2],
        u[0] * v[1] - u[1] * v[0],
    )


def dot3(a, b):
    return a[0] * b[0] + a[1] * b[1] + a[2] * b[2]


def frame(geo, origin):
    corner = [geo[c] - origin[c] for c in range(3)]
    u = [geo[3 + c] for c in range(3)]
    v = [geo[6 + c] for c in range(3)]
    centre = [corner[c] + 0.5 * (u[c] + v[c]) for c in range(3)]
    e1 = [0.25 * (u[c] + v[c]) for c in range(3)]
    e2 = [0.25 * (u[c] - v[c]) for c in range(3)]
    cross = cross_of(u, v)
    area = jnp.sqrt(dot3(cross, cross))
    normal = [cross[c] / area for c in range(3)]
    offsets = [e1, [-x for x in e1], e2, [-x for x in e2]]
    return centre, offsets, normal, area


def across(row):
    parts = [
        jnp.transpose(jnp.broadcast_to(row[:, c : c + 128], (128, 128)))
        for c in range(0, row.shape[1], 128)
    ]
    return jnp.concatenate(parts, 0)


def recv_kernel(geo_ref, refl, left0, left1, left2, centres, refl_out, middle_out):
    geo = [geo_ref[c : c + 1] for c in range(9)]
    origin = [jnp.mean(geo[c], 1, keepdims=True) for c in range(3)]
    middle_out[...] = jnp.concatenate(
        [jnp.broadcast_to(x, (1, LANES)) for x in origin] + [jnp.zeros((5, LANES), F32)], 0
    )
    centre, offsets, normal, _ = frame(geo, origin)
    one = jnp.ones_like(centre[0])
    zero = jnp.zeros_like(one)

    def columns(rows):
        hi, mid, lo = split3(jnp.concatenate(rows, 0))
        pad = [jnp.zeros_like(hi)] * ((128 - SPLIT_K) // 8)
        wide = jnp.concatenate([hi, hi, hi, mid, mid, lo] + pad, 0)
        return jnp.transpose(wide)[:, :SPLIT_K].astype(BF16)

    for p, a in enumerate(offsets):
        point = [centre[c] + a[c] for c in range(3)]
        cols0 = columns(point + [dot3(point, point), one] + [zero] * 3)
        cols1 = columns(point + list(a) + [one, dot3(a, a) + 2.0 * dot3(centre, a)])
        for c in range(left1.shape[0]):
            rows = slice(c * CH, (c + 1) * CH)
            left0[c, p * CH : (p + 1) * CH, :] = cols0[rows]
            left1[c, p * CH : (p + 1) * CH, :] = cols1[rows]
    left2[...] = columns(list(normal) + [-dot3(normal, centre)] + [zero] * 4)
    for c in range(3):
        centres[c] = across(centre[c])
    refl_out[...] = refl[...]


def recv_factors(geometry, reflect):
    width = geometry.shape[1]
    vmem = pl.BlockSpec(memory_space=pltpu.VMEM)
    return pl.pallas_call(
        recv_kernel,
        out_shape=(
            jax.ShapeDtypeStruct((width // CH, 4 * CH, SPLIT_K), BF16),
            jax.ShapeDtypeStruct((width // CH, 4 * CH, SPLIT_K), BF16),
            jax.ShapeDtypeStruct((width, SPLIT_K), BF16),
            jax.ShapeDtypeStruct((3, width, 128), F32),
            jax.ShapeDtypeStruct((1, width), F32),
            jax.ShapeDtypeStruct((8, LANES), F32),
        ),
        in_specs=[vmem] * 2,
        out_specs=(vmem,) * 6,
        cost_estimate=pl.CostEstimate(flops=200000, bytes_accessed=1600000, transcendentals=1024),
        compiler_params=pltpu.CompilerParams(vmem_limit_bytes=4 << 20),
        name="recv_factors",
    )(geometry, reflect)


def pack_kernel(
    count, recv_h, src_h, geo_h, emis_h, occ_h, shared, words,
    recv, src, geo, emis, occ, sem,
):
    chunks = emis.shape[1] // LANES
    own = emis.shape[1] // TILE
    me = lax.axis_index("row")
    copies = [
        pltpu.make_async_copy(a, b, sem.at[i])
        for i, (a, b) in enumerate(
            ((recv_h, recv), (src_h, src), (geo_h, geo), (emis_h, emis), (occ_h, occ))
        )
    ]
    for copy in copies:
        copy.start()
    words[...] = jnp.zeros_like(words)
    for copy in copies:
        copy.wait()
    for c in range(chunks):
        lanes = slice(c * LANES, (c + 1) * LANES)
        shared[c * HOURS : (c + 1) * HOURS, :] = emis[:, lanes]
        start = chunks * HOURS + c * SHARED
        shared[start : start + 9, :] = geo[:, lanes]
        shared[start + 9 : start + 10, :] = jnp.zeros((1, LANES), F32)
    lane = lax.broadcasted_iota(jnp.int32, (1, LANES), 1)

    def slot(k, code):
        tile = recv[k]
        owner = tile // own
        row = 2 * (tile - owner * own)
        line = occ[pl.ds(k, 1), :].astype(F32)
        for c in range(2):
            words[owner ^ me, pl.ds(row + c, 1), :] = line[:, c * LANES : (c + 1) * LANES]
        return jnp.where(lane == tile, 1 + src[k], code)

    code = lax.fori_loop(0, count[0], slot, jnp.zeros_like(lane))
    start = chunks * HOURS + 9
    shared[start : start + 1, :] = code.astype(F32)


def pack(geometry, emission, occlusion, pair_recv, pair_src, pair_count):
    vmem = pl.BlockSpec(memory_space=pltpu.VMEM)
    smem = pl.BlockSpec(memory_space=pltpu.SMEM)
    hbm = pl.BlockSpec(memory_space=pltpu.HBM)
    width = geometry.shape[1]
    n_dev = lax.axis_size("row")
    large = [
        pltpu.with_memory_space_constraint(x, pltpu.HBM)
        for x in (pair_recv, pair_src, geometry, emission, occlusion)
    ]
    return pl.pallas_call(
        pack_kernel,
        out_shape=(
            jax.ShapeDtypeStruct((width // LANES * (HOURS + SHARED), LANES), F32),
            jax.ShapeDtypeStruct((n_dev, width // LANES, LANES), F32),
        ),
        in_specs=[smem] + [hbm] * 5,
        out_specs=(vmem, vmem),
        scratch_shapes=[
            pltpu.SMEM(pair_recv.shape, jnp.int32),
            pltpu.SMEM(pair_src.shape, jnp.int32),
            pltpu.VMEM(geometry.shape, F32),
            pltpu.VMEM(emission.shape, F32),
            pltpu.VMEM(occlusion.shape, jnp.int32),
            pltpu.SemaphoreType.DMA((5,)),
        ],
        compiler_params=pltpu.CompilerParams(vmem_limit_bytes=4 << 20),
        name="pack",
    )(pair_count, *large)


def source_factors(geo, origin, exact, rhs1, rhs2, middle):
    centre, offsets, normal, area = frame(geo, origin)
    one = jnp.ones_like(area)
    zero = jnp.zeros_like(area)

    def put(ref, col, rows):
        hi, mid, lo = split3(jnp.concatenate(rows, 0))
        ref[:, col * TILE : (col + 1) * TILE] = jnp.concatenate(
            [hi, mid, lo, hi, mid, hi], 0
        ).astype(BF16)

    if exact:
        m2 = [-2.0 * x for x in centre]
        for q, b in enumerate(offsets):
            rest = dot3(b, b) + 2.0 * dot3(centre, b) + 0.25 * area
            put(rhs1, q, [-2.0 * x for x in b] + m2 + [rest, one])
        put(rhs1, 4, list(normal) + [zero] * 3 + [-dot3(normal, centre), zero])
    else:
        for q, b in enumerate(offsets):
            point = [centre[c] + b[c] for c in range(3)]
            rest = dot3(point, point) + 0.25 * area
            put(rhs1, q, [-2.0 * x for x in point] + [one, rest] + [zero] * 3)
        put(rhs1, 4, list(normal) + [zero, -dot3(normal, centre)] + [zero] * 3)
    weight = area * (1.0 / (16.0 * math.pi))
    for q, b in enumerate(offsets):
        put(
            rhs2,
            q,
            [(centre[c] + b[c]) * weight for c in range(3)] + [weight] + [zero] * 4,
        )
    if exact:
        for c in range(3):
            middle[c : c + 1, :] = centre[c]


def mm(a, b):
    return lax.dot_general(a, b, (((1,), (0,)), ((), ())), preferred_element_type=F32)


def mm_t(a, b):
    return lax.dot_general(a, b, (((1,), (1,)), ((), ())), preferred_element_type=F32)


def inverse_square(t):
    return 1.0 / (t * t)


def block_kernel(
    begin, last, pay, words, left0, left1, left2, centres, refl, origin_ref, *refs
):
    if begin:
        so_far_hi, so_far_lo, *refs = refs
    blocks, order, *refs = refs
    if last:
        out_b, out_sums, out_scale, *refs = refs
    acc_hi, acc_lo, *refs = refs
    (
        rhs1, rhs2, middle, next1, next2, next_middle, word_s, code_v, code, code_sem,
    ) = refs
    n_dev = pay.shape[0]
    own = refl.shape[1] // TILE
    pairs = own * n_dev
    chunks = refl.shape[1] // LANES
    geo_row = chunks * HOURS
    origin = [origin_ref[c : c + 1, 0:1] for c in range(3)]
    lane = lax.broadcasted_iota(jnp.int32, (1, LANES), 1)
    first = own * lax.axis_index("row")
    wide = lax.broadcasted_iota(jnp.int32, (n_dev, LANES), 1)
    table = jnp.zeros((n_dev, LANES), F32)
    rows = pay[:, geo_row + 9, :]
    for r in range(own):
        here = jnp.sum(jnp.where(lane == first + r, rows, 0.0), 1, keepdims=True)
        table = jnp.where(wide == r, here, table)
    far = [jnp.zeros((n_dev, LANES), F32)] * 3
    for c in range(chunks):
        for part in range(3):
            at = geo_row + SHARED * c + 3 * part
            v = [pay[:, at + x, :] for x in range(3)]
            if part == 0:
                v = [v[x] - origin[x] for x in range(3)]
            far[part] = jnp.maximum(far[part], dot3(v, v))
    reach = sum(jnp.sqrt(jnp.max(f)) for f in far)
    near = 2.0 * reach * reach * 2.0**-23 <= NEAR * 0.25 * AREA_MIN
    code_v[...] = table.astype(jnp.int32)
    to_scalar = pltpu.make_async_copy(code_v, code, code_sem)
    to_scalar.start()
    acc_hi[...] = so_far_hi[...] if begin else jnp.zeros_like(acc_hi)
    acc_lo[...] = so_far_lo[...] if begin else jnp.zeros_like(acc_lo)
    lane = lax.broadcasted_iota(jnp.int32, (1, TILE), 1)
    group_bit = jnp.left_shift(1, lane // (TILE // GROUPS))
    to_scalar.wait()

    order[0] = 0

    n = jnp.int32(0)
    for r in range(own):

        def listed(j, count):
            value = code[j, r]
            order[1 + count] = jnp.maximum(value - 1, 0) * pairs + r * n_dev + j
            return count + (value > 0).astype(jnp.int32)

        n = lax.fori_loop(begin, n_dev, listed, n, unroll=4)
    order[0] = n
    order[1 + n] = 0

    def where_is(i):
        entry = order[1 + i]
        value = entry // pairs
        k = entry - value * pairs
        r = k // n_dev
        return r, k - r * n_dev, value

    def prepare(i, exact):
        _, j, source = where_is(i)
        at = geo_row + 2 * SHARED * source
        geo = [
            jnp.concatenate(
                [pay[j, pl.ds(at + c, 1), :], pay[j, pl.ds(at + SHARED + c, 1), :]], 1
            )
            for c in range(9)
        ]
        source_factors(geo, origin, exact, next1, next2, next_middle)

    def deposit(i, real):
        i = jnp.maximum(i, 0)
        r, j, source = where_is(i)
        at = pl.multiple_of(2 * HOURS * source, HOURS)
        x = jnp.concatenate(
            [pay[j, pl.ds(at, HOURS), :], pay[j, pl.ds(at + HOURS, HOURS), :]], 1
        )
        x_hi, x_lo = split2(x)
        ones = jnp.ones((16, TILE), BF16)
        hi = mm_t(jnp.concatenate([x_hi, x_lo, ones], 0), blocks[i, 0])
        lo = mm_t(jnp.concatenate([x_hi, ones], 0), blocks[i, 1])
        acc_hi[r] += jnp.where(real, hi, 0.0)
        acc_lo[r] += jnp.where(real, lo, 0.0)

    def pair(exact, i, carry):
        r, j, _ = where_is(i)
        rhs1[...] = next1[...]
        rhs2[...] = next2[...]
        if exact:
            middle[...] = next_middle[...]
        for c in range(2):
            word_s[c * LANES : (c + 1) * LANES, :] = across(
                words[j, pl.ds(2 * r + c, 1), :].astype(jnp.int32)
            )
        deposit(i - 1, i > 0)
        prepare(i + 1, exact)
        for c in range(N_CH):
            rows = slice(c * CH, (c + 1) * CH)
            own_rows = pl.ds(pl.multiple_of(r * TILE + c * CH, CH), CH)
            lhs2 = left2[own_rows, :]
            lhs1 = (left1 if exact else left0)[r * N_CH + c]
            s = None
            for x in range(3 if exact else 0):
                mine = centres[x, own_rows, :]
                d = middle[x : x + 1, :] - jnp.concatenate([mine, mine], 1)
                s = d * d if s is None else s + d * d
            facing = jnp.maximum(mm(lhs1, rhs1[:, 4 * TILE : 5 * TILE]), 0.0)
            total = None
            for q in range(4):
                cols = slice(q * TILE, (q + 1) * TILE)
                rest = mm(lhs1, rhs1[:, cols])
                part = None
                for p in range(4):
                    pr = slice(p * CH, (p + 1) * CH)
                    t = s + rest[pr] if exact else rest[pr]
                    term = facing[pr] * inverse_square(t)
                    part = term if part is None else part + term
                a = jnp.maximum(mm(lhs2, rhs2[:, cols]), 0.0) * part
                total = a if total is None else total + a
            w = word_s[rows, :]
            w = jnp.concatenate([w, w], 1)
            total = jnp.where((w & group_bit) != 0, total, 0.0)
            hi, lo = split2(total)
            blocks[i, 0, rows, :] = hi
            blocks[i, 1, rows, :] = lo
        return carry

    for exact in (False, True):

        @pl.when(jnp.logical_not(near) if exact else near)
        def _():
            prepare(0, exact)
            lax.fori_loop(0, n, functools.partial(pair, exact), 0)

    deposit(n - 1, n > 0)
    if not last:
        return
    for r in range(own):
        cols = slice(r * TILE, (r + 1) * TILE)
        irr = acc_hi[r, 0:16] + acc_hi[r, 16:32] + acc_lo[r, 0:16]
        sums = acc_hi[r, 32:33] + acc_lo[r, 16:17]
        scale = refl[:, cols] / jnp.maximum(sums, 1.0)
        out_sums[:, cols] = sums
        out_scale[:, cols] = scale
        emis = [pay[0, c * HOURS : (c + 1) * HOURS, :] for c in (2 * r, 2 * r + 1)]
        out_b[:, cols] = jnp.concatenate(emis, 1) + scale * irr


def view_blocks(begin, last, pay, words, left, so_far):
    vmem = pl.BlockSpec(memory_space=pltpu.VMEM)
    n_dev = pay.shape[0]
    width = left[4].shape[1]
    own = width // TILE
    pairs = own * n_dev
    sums = [
        jax.ShapeDtypeStruct((own, 48, TILE), F32),
        jax.ShapeDtypeStruct((own, 32, TILE), F32),
    ]
    outs = [
        jax.ShapeDtypeStruct((own * (n_dev - begin), 2, TILE, TILE), BF16),
        jax.ShapeDtypeStruct((2 * pairs,), jnp.int32),
    ]
    scratch = []
    if not last:
        outs += sums
    else:
        outs += [jax.ShapeDtypeStruct((x, width), F32) for x in (HOURS, 1, 1)]
        scratch += [pltpu.VMEM(x.shape, F32) for x in sums]
    args = [pay, words, *left, *so_far]
    work = own * (n_dev - begin) // 2
    return pl.pallas_call(
        functools.partial(block_kernel, begin, last),
        out_shape=outs,
        in_specs=[vmem] * len(args),
        out_specs=[vmem, pl.BlockSpec(memory_space=pltpu.SMEM)] + [vmem] * (len(outs) - 2),
        scratch_shapes=scratch
        + [
            pltpu.VMEM((SPLIT_K, 5 * TILE), BF16),
            pltpu.VMEM((SPLIT_K, 4 * TILE), BF16),
            pltpu.VMEM((8, TILE), F32),
            pltpu.VMEM((SPLIT_K, 5 * TILE), BF16),
            pltpu.VMEM((SPLIT_K, 4 * TILE), BF16),
            pltpu.VMEM((8, TILE), F32),
            pltpu.VMEM((TILE, 128), jnp.int32),
            pltpu.VMEM((n_dev, 128), jnp.int32),
            pltpu.SMEM((n_dev, 128), jnp.int32),
            pltpu.SemaphoreType.DMA,
        ],
        compiler_params=pltpu.CompilerParams(vmem_limit_bytes=12 << 20),
        cost_estimate=pl.CostEstimate(
            flops=work * 10**9, bytes_accessed=work << 18, transcendentals=work << 20
        ),
        name="view_blocks",
    )(*args)


def bounce_kernel(last, field, blocks, order, *refs):
    if last:
        so_far, scale, emis, out, acc = refs
        acc[...] = so_far[...]
    else:
        (acc,) = refs
        acc[...] = jnp.zeros_like(acc)
    own = acc.shape[0]

    def some(order, blocks, step, carry):
        pairs = order.shape[0] // 2
        n_dev = pairs // own
        for b in range(4):
            i = 4 * step + b
            live = i < order[0]
            entry = jnp.where(live, order[jnp.minimum(1 + i, 2 * pairs - 1)], 0)
            source = entry // pairs
            k = entry - source * pairs
            r = k // n_dev
            j = k - r * n_dev
            at = jnp.minimum(i, blocks.shape[0] - 1)
            lanes = pl.ds(pl.multiple_of(source * TILE, TILE), TILE)
            x_hi, x_lo = split2(field[j, :, lanes])
            both = mm_t(jnp.concatenate([x_hi, x_lo], 0), blocks[at, 0])
            got = both[0:16] + both[16:32] + mm_t(x_hi, blocks[at, 1])
            acc[r] += jnp.where(live, got, 0.0)
        return carry

    lax.fori_loop(0, (order[0] + 3) // 4, functools.partial(some, order, blocks), 0)
    for r in range(own if last else 0):
        cols = slice(r * TILE, (r + 1) * TILE)
        out[:, cols] = emis[:, cols] + scale[:, cols] * acc[r]


def bounce(last, field, blocks, order, *rest):
    vmem = pl.BlockSpec(memory_space=pltpu.VMEM)
    own = field.shape[2] // TILE
    sums = (own, HOURS, TILE)
    out = (HOURS, field.shape[2]) if last else sums
    work = blocks.shape[0] // 2
    return pl.pallas_call(
        functools.partial(bounce_kernel, last),
        out_shape=jax.ShapeDtypeStruct(out, F32),
        in_specs=[vmem, vmem, pl.BlockSpec(memory_space=pltpu.SMEM)] + [vmem] * len(rest),
        out_specs=vmem,
        scratch_shapes=[pltpu.VMEM(sums, F32)] if last else [],
        compiler_params=pltpu.CompilerParams(vmem_limit_bytes=12 << 20),
        cost_estimate=pl.CostEstimate(
            flops=work * 10**8, bytes_accessed=work << 18, transcendentals=0
        ),
        name="second_bounce",
    )(field, blocks, order, *rest)


def on_device(geometry, emission, reflect, occlusion, pair_recv, pair_src, pair_count):
    n_dev = lax.axis_size("row")
    shared, words = pack(geometry, emission, occlusion, pair_recv, pair_src, pair_count)
    left = recv_factors(geometry, reflect[None])
    held, words = shared[None], words[None]
    done, so_far, begin = [], [], 0
    step = n_dev // 2
    while step:
        lines = held.shape[0] * held.shape[1]
        keep, send = words[:, :step], words[:, step:]
        message = jnp.concatenate([held.reshape(-1, LANES), send.reshape(-1, LANES)], 0)
        other = lax.ppermute(message, "row", [(i, i ^ step) for i in range(n_dev)])
        if step == n_dev // 2:
            other, left = lax.optimization_barrier((other, left))
        elif step == 2:
            early = view_blocks(begin, False, held, words[:, 0], left, so_far)
            other, early = lax.optimization_barrier((other, early))
            done.append(tuple(early[:2]))
            so_far = early[2:]
            begin = held.shape[0]
        held = jnp.concatenate([held, other[:lines].reshape(held.shape)], 0)
        words = jnp.concatenate([keep, other[lines:].reshape(send.shape)], 0)
        step //= 2
    blocks, order, field, sums, scale = view_blocks(
        begin, True, held, words[:, 0], left, so_far
    )
    done.append((blocks, order))
    fields, step = field[None], n_dev // 2
    while step:
        other = lax.ppermute(fields, "row", [(i, i ^ step) for i in range(n_dev)])
        if step == 2:
            part = bounce(False, fields, *done[0])
            other, part = lax.optimization_barrier((other, part))
        fields = jnp.concatenate([fields, other], 0)
        step //= 2
    radiosity = bounce(True, fields, *done[1], part, scale, emission)
    return (radiosity, sums[0])


def solution(mesh):
    placed = (
        P(None, ("grp", "row")),
        P(None, ("grp", "row")),
        P(("grp", "row")),
        P(("grp", "row"), None),
        P(("grp", "row")),
        P(("grp", "row")),
        P(("grp", "row")),
    )
    return jax.shard_map(
        on_device,
        mesh=mesh,
        in_specs=placed,
        out_specs=(P(None, ("grp", "row")), P(("grp", "row"))),
        check_vma=False,
    )
```
